32 devices in a mesh: dp: 8 (over z, x), band: 4 (over y, core).
Axes of the slice: x: 2, y: 2, z: 4, core: 2. Of those that a mesh axis runs over, the one named last changes fastest.
Arguments:
- inputs: bfloat16 [2, 8, 2048, 768], P(None, 'dp', 'band'), may hold values from -6 to 6
- segments: int32 [2, 8, 2048], P(None, 'dp', 'band'), may hold values from 0 to 6, as said below
- cotangent: bfloat16 [2, 8, 2048, 768], P(None, 'dp', 'band'), may hold values from -6 to 6
- ln1_gain: bfloat16 [768], P('band'), may hold values from 0.5 to 1.5
- ln1_bias: bfloat16 [768], P('band'), may hold values from -3 to 3
- w_qkv: bfloat16 [768, 2304], P('band'), may hold values from -0.21875 to 0.21875
- b_qv: bfloat16 [1536], P('band'), may hold values from -0.4375 to 0.4375
- w_out: bfloat16 [768, 768], P('band'), may hold values from -2.5 to 2.5
- b_out: bfloat16 [768], P('band'), may hold values from -3 to 3
- ln2_gain: bfloat16 [768], P('band'), may hold values from 0.5 to 1.5
- ln2_bias: bfloat16 [768], P('band'), may hold values from -3 to 3
- w_up: bfloat16 [768, 3072], P('band'), may hold values from -0.21875 to 0.21875
- b_up: bfloat16 [3072], P('band'), may hold values from -3 to 3
- w_down: bfloat16 [3072, 768], P('band'), may hold values from -0.109375 to 0.109375
- b_down: bfloat16 [768], P('band'), may hold values from -3 to 3
Outputs:
- output: bfloat16 [2, 8, 2048, 768], P(None, 'dp', 'band')
- input_grad: bfloat16 [2, 8, 2048, 768], P(None, 'dp', 'band')
- grad_ln1_gain: float32 [768], P('band')
- grad_ln1_bias: float32 [768], P('band')
- grad_w_qkv: float32 [768, 2304], P('band')
- grad_b_qv: float32 [1536], P('band')
- grad_w_out: float32 [768, 768], P('band')
- grad_b_out: float32 [768], P('band')
- grad_ln2_gain: float32 [768], P('band')
- grad_ln2_bias: float32 [768], P('band')
- grad_w_up: float32 [768, 3072], P('band')
- grad_b_up: float32 [3072], P('band')
- grad_w_down: float32 [3072, 768], P('band')
- grad_b_down: float32 [768], P('band')
The draws below stay inside these ranges and needn't reach their ends.
Inputs may be any that keep to these rules, and one draw needn't show every extreme that they name: `segments`: each sequence's 2048 slots are consecutive blocks of 512 slots that carry the same ids in the same order. In a block, ids never fall: tiles 1, 2, 3 and so on are contiguous runs, and padding (0) fills the end of the block, at most 51 slots.
All inputs are finite; a program needn't handle non-finite values.
Results may differ from the reference program's by a relative error of at most 0.02.
Values may be sent and summed in bfloat16 or wider, within the bound.
No kernel may reach another device: no remote copies, remote signals or barrier semaphores. Data moves between devices by JAX's collectives and lax.ppermute only.
A program may use at most 192 MiB of HBM per device.

```python
import jax
import jax.numpy as jnp
from jax import lax

HEADS = 12
HD = 64
D = 768
FF = 3072
TOK_DEV = 512
MICRO = 2
SEQ_LEN = 2048
SEQS = 8
N_BAND = 4


def draw_segments(key, part):
    first_key = jax.random.fold_in(key, 11)
    second_key = jax.random.fold_in(key, 23)
    least = TOK_DEV * 3 // 16
    lengths = jax.random.randint(first_key, (MICRO, SEQS, 8), least, TOK_DEV * 3 // 4 + 1)
    lengths = lengths.at[0, 0].set(least)
    padding = jax.random.randint(second_key, (MICRO, SEQS, 1), 0, TOK_DEV // 10 + 1)
    padding = padding.at[0, 0].set(0)
    ends = jnp.cumsum(lengths, axis=-1)
    slots = jnp.arange(TOK_DEV, dtype=jnp.int32)
    tiles = jnp.sum((ends[:, :, None, :] <= slots[None, None, :, None]).astype(jnp.int32), axis=-1)
    block = jnp.where(slots[None, None, :] < TOK_DEV - padding, tiles + 1, 0)
    return jnp.tile(block, (1, 1, N_BAND)).astype(jnp.int32)


def block_levels(rng, extent, split, smallest, high):
    def one(axis_at, parts):
        heights = jax.random.uniform(jax.random.fold_in(jax.random.fold_in(rng, 6), axis_at), (parts,), jnp.float32, smallest / len(split), high / len(split))
        return jnp.repeat(jnp.exp(heights), extent[axis_at] // parts).reshape((-1,) + (1,) * (len(extent) - axis_at - 1))

    level = one(*split[0])
    for cut in split[1:]:
        level = level * one(*cut)
    return level


def gaussian(own_key, shape, scale, reach, cuts=(), kind=jnp.bfloat16):
    values = jax.random.normal(own_key, shape, jnp.float32) * scale
    if len(cuts) > 0:
        values = block_levels(own_key, shape, cuts, -0.22, 0.18) * values
    return jnp.clip(values, min=-reach, max=reach).astype(kind)


def setup_inputs(seed: int = 0) -> dict:
    key_list = jax.random.split(jax.random.key(seed), 16)
    inputs = gaussian(key_list[0], (MICRO, SEQS, SEQ_LEN, D), 1.0, 6.0, ((1, 8), (2, 4)))
    segments = draw_segments(jax.random.fold_in(key_list[15], 71), 0)
    cotangent = gaussian(key_list[2], (MICRO, SEQS, SEQ_LEN, D), 1.0, 6.0, ((1, 8), (2, 4)))
    ln1_gain = jnp.clip(1.0 + 0.1 * jax.random.normal(key_list[3], (D,), jnp.float32), 0.5, 1.5).astype(jnp.bfloat16)
    ln1_bias = gaussian(key_list[4], (D,), 0.2, 3.0, ((0, 4),))
    w_qkv = gaussian(key_list[5], (D, 3 * D), D ** -0.5, 0.21875, ((0, 4),))
    b_qv = gaussian(key_list[6], (2 * D,), 0.03, 0.4375, ((0, 4),))
    w_out = gaussian(key_list[7], (D, D), (max(D // 128, 1)) ** -0.5, 2.5, ((0, 4),))
    b_out = gaussian(key_list[8], (D,), 0.2, 3.0, ((0, 4),))
    ln2_gain = jnp.clip(1.0 + 0.1 * jax.random.normal(key_list[9], (D,), jnp.float32), 0.5, 1.5).astype(jnp.bfloat16)
    ln2_bias = gaussian(key_list[10], (D,), 0.2, 3.0, ((0, 4),))
    w_up = gaussian(key_list[11], (D, FF), D ** -0.5, 0.21875, ((0, 4),))
    b_up = gaussian(key_list[12], (FF,), 0.2, 3.0, ((0, 4),))
    w_down = gaussian(key_list[13], (FF, D), FF ** -0.5, 0.109375, ((0, 4),))
    b_down = gaussian(key_list[14], (D,), 0.2, 3.0, ((0, 4),))
    return {"inputs": inputs, "segments": segments, "cotangent": cotangent, "ln1_gain": ln1_gain, "ln1_bias": ln1_bias, "w_qkv": w_qkv, "b_qv": b_qv, "w_out": w_out, "b_out": b_out, "ln2_gain": ln2_gain, "ln2_bias": ln2_bias, "w_up": w_up, "b_up": b_up, "w_down": w_down, "b_down": b_down}


@jax.custom_vjp
def low(v):
    return lax.optimization_barrier(v.astype(jnp.bfloat16)).astype(jnp.float32)

@jax.custom_vjp
def low_back(v):
    return v

def low_keep(v):
    return (low(v), None)

def low_pass(kept, grad):
    return (grad,)

def back_keep(v):
    return (v, None)

def back_low(kept, grad):
    return (low(grad),)
low.defvjp(low_keep, low_pass)
low_back.defvjp(back_keep, back_low)
highest = lax.Precision.HIGHEST

def normed(value, gain, shift):
    center = value - lax.optimization_barrier(jnp.mean(value, axis=-1, keepdims=True))
    spread = lax.optimization_barrier(jnp.mean(center * center, axis=-1, keepdims=True))
    return center * lax.rsqrt(spread + 1e-06) * gain + shift

def head_attend(query, keys, values, mask):
    scores = low_back(jnp.dot(query, keys.T, precision=highest) * 0.125)
    scores = jnp.where(mask, scores, -1e+30)
    weights = jax.nn.softmax(scores, axis=-1)
    return jnp.dot(low(weights), values, precision=highest)

def layer(inputs, params, segment):
    ln1_gain, ln1_bias, w_qkv, b_qv, w_out, b_out, ln2_gain, ln2_bias, w_up, b_up, w_down, b_down = params
    length = inputs.shape[0]
    normed_in = low(normed(inputs, ln1_gain, ln1_bias))
    projected = jnp.dot(normed_in, w_qkv, precision=highest)
    query = low_back(low(projected[:, :D] + b_qv[:D]))
    keys = low_back(low(projected[:, D:2 * D]))
    values = low_back(low(projected[:, 2 * D:] + b_qv[D:]))
    mask = segment[:, None] == segment[None, :]

    def split_heads(block):
        return block.reshape(length, HEADS, HD).transpose(1, 0, 2)
    attend = jax.checkpoint(lambda item: head_attend(item[0], item[1], item[2], mask))
    heads_out = lax.map(attend, (split_heads(query), split_heads(keys), split_heads(values)))
    mixed = low_back(low(heads_out.transpose(1, 0, 2).reshape(length, D)))
    hidden = inputs + low_back(jnp.dot(mixed, w_out, precision=highest) + b_out)
    normed_mid = low(normed(hidden, ln2_gain, ln2_bias))
    upward = low_back(jnp.dot(normed_mid, w_up, precision=highest) + b_up)
    active = low(jax.nn.gelu(upward, approximate=True))
    return hidden + low_back(jnp.dot(active, w_down, precision=highest) + b_down)

def reference(inputs, segments, cotangent, ln1_gain, ln1_bias, w_qkv, b_qv, w_out, b_out, ln2_gain, ln2_bias, w_up, b_up, w_down, b_down):
    params = tuple((param.astype(jnp.float32) for param in (ln1_gain, ln1_bias, w_qkv, b_qv, w_out, b_out, ln2_gain, ln2_bias, w_up, b_up, w_down, b_down)))
    count = MICRO * SEQS
    flat_in = inputs.astype(jnp.float32).reshape(count, SEQ_LEN, D)
    flat_seg = segments.reshape(count, SEQ_LEN)
    flat_cot = cotangent.astype(jnp.float32).reshape(count, SEQ_LEN, D)

    def step(totals, item):
        sample, segment, grad_given = item
        result, pull = jax.vjp(lambda value, weights: layer(value, weights, segment), sample, params)
        grad_out = grad_given * (segment != 0).astype(jnp.float32)[:, None]
        grad_in, grad_weights = pull(grad_out)
        totals = tuple((first + second for first, second in zip(totals, grad_weights)))
        return (totals, (result.astype(jnp.bfloat16), grad_in.astype(jnp.bfloat16)))
    start = tuple((jnp.zeros(param.shape, jnp.float32) for param in params))
    totals, (results, grads_in) = lax.scan(step, start, (flat_in, flat_seg, flat_cot))
    return (results.reshape(MICRO, SEQS, SEQ_LEN, D), grads_in.reshape(MICRO, SEQS, SEQ_LEN, D), totals[0], totals[1], totals[2], totals[3], totals[4], totals[5], totals[6], totals[7], totals[8], totals[9], totals[10], totals[11])
```

```python
import functools

import jax
import jax.numpy as jnp
from jax import lax
from jax.sharding import PartitionSpec as P
from jax.experimental import pallas as pl
from jax.experimental.pallas import tpu as pltpu
bf=jnp.bfloat16; f32=jnp.float32
HD=64
def nt(a,b): return lax.dot_general(a,b,(((1,),(1,)),((),())),preferred_element_type=f32)
def nn(a,b): return lax.dot_general(a,b,(((1,),(0,)),((),())),preferred_element_type=f32)
def tn(a,b): return lax.dot_general(a,b,(((0,),(0,)),((),())),preferred_element_type=f32)
def lanes(shape): return lax.broadcasted_iota(jnp.int32,shape,1)
NEG=-1e30

def mask_feats_q(seg, base):
    l=lanes((seg.shape[0],2*HD))
    return (l==seg+base).astype(f32)
def mask_feats_k(seg, base):
    l=lanes((seg.shape[0],2*HD))
    inr=(l>=base)&(l<base+8)
    return jnp.where(inr&(l!=seg+base),NEG,0.0)

def fwd_kernel(q_ref,k_ref,v_ref,segq_ref,segk_ref,o_ref,lse_ref,*,tq):
    n=q_ref.shape[0]
    k=k_ref[...]; v=v_ref[...]
    segk=segk_ref[...]
    lk=lanes(k.shape)<HD
    ks=[jnp.where(lk,k,mask_feats_k(segk,HD).astype(bf)),
        jnp.where(lk,mask_feats_k(segk,0).astype(bf),k)]
    for t in range(n//tq):
        rows=pl.ds(t*tq,tq)
        q=q_ref[rows,:]*jnp.asarray(0.125,bf)
        lq=lanes(q.shape)<HD
        segq=segq_ref[rows,:]
        outs=[];lses=[]
        for h in range(2):
            qq=jnp.where(lq,q,mask_feats_q(segq,HD).astype(bf)) if h==0 else jnp.where(lq,mask_feats_q(segq,0).astype(bf),q)
            s=nt(qq,ks[h])
            m=jnp.max(s,axis=-1,keepdims=True)
            p=jnp.exp(s-m)
            l=jnp.sum(p,axis=-1,keepdims=True)
            o=nn(p.astype(bf),v)
            outs.append(o/l); lses.append(m+jnp.log(l))
        o_ref[rows,:]=jnp.where(lq,outs[0],outs[1]).astype(bf)
        lse_ref[rows,:]=jnp.where(lq,jnp.broadcast_to(lses[0],q.shape),jnp.broadcast_to(lses[1],q.shape))

def attn_fwd(q,k,v,segq,segk,tq=256):
    n,d=q.shape; m=k.shape[0]
    pairs=d//(2*HD)
    col=lambda r: pl.BlockSpec((r,2*HD),lambda h:(0,h))
    full=lambda r: pl.BlockSpec((r,1),lambda h:(0,0))
    return pl.pallas_call(functools.partial(fwd_kernel,tq=tq),grid=(pairs,),
        in_specs=[col(n),col(m),col(m),full(n),full(m)],
        out_specs=[col(n),col(n)],
        out_shape=[jax.ShapeDtypeStruct((n,d),bf),jax.ShapeDtypeStruct((n,d),f32)],
        name="attn_fwd")(q,k,v,segq[:,None],segk[:,None])

def bwd_kernel(q_ref,k_ref,v_ref,do_ref,o_ref,lse_ref,segq_ref,segk_ref,dq_ref,dk_ref,dv_ref,*,tq,tk):
    n=q_ref.shape[0]; mkeys=k_ref.shape[0]
    for c in range(mkeys//tk):
        kr=pl.ds(c*tk,tk)
        k=k_ref[kr,:]; v=v_ref[kr,:]; segk=segk_ref[kr,:]
        lk=lanes(k.shape)<HD
        z=jnp.zeros_like(k)
        ks=[jnp.where(lk,k,mask_feats_k(segk,HD).astype(bf)), jnp.where(lk,mask_feats_k(segk,0).astype(bf),k)]
        km=[jnp.where(lk,k,z),jnp.where(lk,z,k)]
        dk=jnp.zeros((tk,2*HD),f32); dv=jnp.zeros((tk,2*HD),f32)
        for t in range(n//tq):
            rows=pl.ds(t*tq,tq)
            q=q_ref[rows,:]*jnp.asarray(0.125,bf); do=do_ref[rows,:]
            lq=lanes(q.shape)<HD
            zq=jnp.zeros_like(q)
            segq=segq_ref[rows,:]
            lse=lse_ref[rows,:]
            prod=do.astype(f32)*o_ref[rows,:].astype(f32)
            dqs=None
            for h in range(2):
                own=lq if h==0 else ~lq
                qq=jnp.where(own,q,mask_feats_q(segq,HD if h==0 else 0).astype(bf))
                qm=jnp.where(own,q,zq); dom=jnp.where(own,do,zq)
                dd=jnp.sum(jnp.where(own,prod,0.0),axis=-1,keepdims=True)
                ls=lse[:,:1] if h==0 else lse[:,HD:HD+1]
                p=jnp.exp(nt(qq,ks[h])-ls)
                dp=nt(dom,v)
                ds=(p*(dp-dd)).astype(bf)
                dv=dv+tn(p.astype(bf),dom)
                dk=dk+tn(ds,qm)
                x=nn(ds,km[h])
                dqs=x if dqs is None else dqs+x
            dqs=dqs*0.125
            if c==0: dq_ref[rows,:]=dqs
            else: dq_ref[rows,:]+=dqs
        dk_ref[kr,:]=dk.astype(bf); dv_ref[kr,:]=dv.astype(bf)

def attn_bwd(q,k,v,do,o,lse,segq,segk,tq=256,tk=1024):
    n,d=q.shape; m=k.shape[0]
    pairs=d//(2*HD)
    col=lambda r: pl.BlockSpec((r,2*HD),lambda h:(0,h))
    full=lambda r: pl.BlockSpec((r,1),lambda h:(0,0))
    return pl.pallas_call(functools.partial(bwd_kernel,tq=tq,tk=tk),grid=(pairs,),
        in_specs=[col(n),col(m),col(m),col(n),col(n),col(n),full(n),full(m)],
        out_specs=[col(n),col(m),col(m)],
        out_shape=[jax.ShapeDtypeStruct((n,d),f32),jax.ShapeDtypeStruct((m,d),bf),jax.ShapeDtypeStruct((m,d),bf)],
        name="attn_bwd")(q,k,v,do,o,lse,segq[:,None],segk[:,None])


def normed(value, gain, shift):
    center = value - jnp.mean(value, axis=-1, keepdims=True)
    spread = jnp.mean(center * center, axis=-1, keepdims=True)
    return center * lax.rsqrt(spread + 1e-06) * gain + shift


def gelu_tanh(value):
    return jax.nn.gelu(value, approximate=True)


def swap(x, flip):
    parts = lax.axis_size("band")
    return lax.ppermute(x, "band", [(i, i ^ flip) for i in range(parts)])


def gather_relative(x):
    flip = lax.axis_size("band") // 2
    while flip >= 1:
        x = jnp.concatenate([x, swap(x, flip)], axis=0)
        flip //= 2
    return x


def reduce_relative(x):
    flip = 1
    while flip < lax.axis_size("band"):
        half = x.shape[0] // 2
        x = (x[:half].astype(f32) + swap(x[half:], flip).astype(f32)).astype(bf)
        flip *= 2
    return x


VECTORS = ("ln1_gain", "ln1_bias", "b_qv", "b_out", "ln2_gain", "ln2_bias", "b_up", "b_down")


def gather_vectors(shards):
    parts = lax.axis_size("band")
    packed = jnp.concatenate(shards)
    whole = lax.all_gather(packed, "band", axis=0, tiled=False)
    out, at = [], 0
    for shard in shards:
        out.append(whole[:, at : at + shard.shape[0]].reshape(-1).astype(f32))
        at += shard.shape[0]
    return out


def reduce_vectors(grads, shards):
    parts = lax.axis_size("band")
    packed = jnp.concatenate([g.reshape(parts, -1) for g in grads], axis=1).astype(bf)
    total = lax.psum(packed, ("dp", "band"))
    mine = lax.dynamic_index_in_dim(total, lax.axis_index("band"), 0, keepdims=False).astype(f32)
    out, at = [], 0
    for shard in shards:
        out.append(mine[at : at + shard.shape[0]])
        at += shard.shape[0]
    return out


def gather_matrix(shard):
    return lax.all_gather(shard, "band", axis=0, tiled=True)


def reduce_matrix(grad):
    part = lax.psum_scatter(grad.astype(bf), "band", scatter_dimension=0, tiled=True)
    return lax.psum(part, "dp").astype(f32)


def body(inputs, segments, cotangent, ln1_gain, ln1_bias, w_qkv, b_qv, w_out, b_out, ln2_gain, ln2_bias, w_up, b_up, w_down, b_down):
    micro, tokens, width = inputs.shape[0], inputs.shape[2], inputs.shape[3]
    parts = lax.axis_size("band")
    vectors = (ln1_gain, ln1_bias, b_qv, b_out, ln2_gain, ln2_bias, b_up, b_down)
    gain_one, shift_one, bias_qv, bias_out, gain_two, shift_two, bias_up, bias_down = gather_vectors(vectors)
    w_proj = gather_matrix(w_qkv)
    w_mix = gather_matrix(w_out)
    w_rise = gather_matrix(w_up)
    w_fall = gather_matrix(w_down)

    value = inputs.reshape(micro * tokens, width).astype(f32)
    seg = segments.reshape(micro, tokens)
    normed_in, pull_one = jax.vjp(normed, value, gain_one, shift_one)
    normed_low = normed_in.astype(bf)
    projected = nn(normed_low, w_proj)
    query = (projected[:, :width] + bias_qv[:width]).astype(bf)
    keys = projected[:, width : 2 * width].astype(bf)
    values = (projected[:, 2 * width :] + bias_qv[width:]).astype(bf)

    saved, mixes = [], []
    for m in range(micro):
        rows = slice(m * tokens, (m + 1) * tokens)
        keys_all = gather_relative(keys[rows])
        values_all = gather_relative(values[rows])
        seg_keys = jnp.tile(seg[m], parts)
        mix, log_total = attn_fwd(query[rows], keys_all, values_all, seg[m], seg_keys)
        mixes.append(mix)
        saved.append((query[rows], keys_all, values_all, mix, log_total, seg[m], seg_keys))
    mixed = jnp.concatenate(mixes)

    hidden = value + (nn(mixed, w_mix) + bias_out)
    normed_mid, pull_two = jax.vjp(normed, hidden, gain_two, shift_two)
    mid_low = normed_mid.astype(bf)
    upward = nn(mid_low, w_rise) + bias_up
    active, pull_gelu = jax.vjp(gelu_tanh, upward)
    active_low = active.astype(bf)
    output = (hidden + (nn(active_low, w_fall) + bias_down)).astype(bf)

    real = (seg.reshape(-1, 1) != 0).astype(f32)
    grad_y = cotangent.reshape(micro * tokens, width).astype(f32) * real
    grad_m = grad_y.astype(bf)
    grad_w_fall = tn(active_low, grad_m)
    grad_b_fall = jnp.sum(grad_m.astype(f32), axis=0)
    grad_up = pull_gelu(nt(grad_m, w_fall))[0].astype(bf)
    grad_w_rise = tn(mid_low, grad_up)
    grad_b_rise = jnp.sum(grad_up.astype(f32), axis=0)
    grad_mid, grad_gain_two, grad_shift_two = pull_two(nt(grad_up, w_rise))
    grad_hidden = grad_y + grad_mid
    grad_a = grad_hidden.astype(bf)
    grad_w_mix = tn(mixed, grad_a)
    grad_b_mix = jnp.sum(grad_a.astype(f32), axis=0)
    grad_mixed = nt(grad_a, w_mix).astype(bf)

    pieces = []
    for m in range(micro):
        rows = slice(m * tokens, (m + 1) * tokens)
        q, k, v, mix, log_total, seg_q, seg_k = saved[m]
        grad_q, grad_k, grad_v = attn_bwd(q, k, v, grad_mixed[rows], mix, log_total, seg_q, seg_k)
        pieces.append(
            jnp.concatenate([grad_q.astype(bf), reduce_relative(grad_k), reduce_relative(grad_v)], axis=1)
        )
    grad_qkv = jnp.concatenate(pieces)
    grad_w_proj = tn(normed_low, grad_qkv)
    sums = jnp.sum(grad_qkv.astype(f32), axis=0)
    grad_b_proj = jnp.concatenate([sums[:width], sums[2 * width :]])
    grad_norm_in, grad_gain_one, grad_shift_one = pull_one(nt(grad_qkv, w_proj))
    input_grad = (grad_hidden + grad_norm_in).astype(bf)

    small = reduce_vectors(
        (grad_gain_one, grad_shift_one, grad_b_proj, grad_b_mix, grad_gain_two, grad_shift_two, grad_b_rise, grad_b_fall),
        vectors,
    )
    return (
        output.reshape(inputs.shape),
        input_grad.reshape(inputs.shape),
        small[0],
        small[1],
        reduce_matrix(grad_w_proj),
        small[2],
        reduce_matrix(grad_w_mix),
        small[3],
        small[4],
        small[5],
        reduce_matrix(grad_w_rise),
        small[6],
        reduce_matrix(grad_w_fall),
        small[7],
    )


def solution(mesh):
    split = P(None, "dp", "band", None)
    rows, vector = P("band", None), P("band")
    weights = (vector, vector, rows, vector, rows, vector, vector, vector, rows, vector, rows, vector)
    return jax.shard_map(
        body,
        mesh=mesh,
        in_specs=(split, P(None, "dp", "band"), split) + weights,
        out_specs=(split, split) + weights,
        check_vma=False,
    )
```

```python
import functools

import jax
import jax.numpy as jnp
from jax import lax
from jax.sharding import PartitionSpec as P
from jax.experimental import pallas as pl
from jax.experimental.pallas import tpu as pltpu
bf=jnp.bfloat16; f32=jnp.float32
HD=64


def nt(a,b): return lax.dot_general(a,b,(((1,),(1,)),((),())),preferred_element_type=f32)


def nn(a,b): return lax.dot_general(a,b,(((1,),(0,)),((),())),preferred_element_type=f32)


def tn(a,b): return lax.dot_general(a,b,(((0,),(0,)),((),())),preferred_element_type=f32)


def lanes(shape): return lax.broadcasted_iota(jnp.int32,shape,1)


NEG=-1e30


def mask_feats_q(seg, base):
    l=lanes((seg.shape[0],2*HD))
    return (l==seg+base).astype(f32)


def mask_feats_k(seg, base):
    l=lanes((seg.shape[0],2*HD))
    inr=(l>=base)&(l<base+8)
    return jnp.where(inr&(l!=seg+base),NEG,0.0)


def both_masks(k, segk):
    low = lanes(k.shape) < HD
    return [
        jnp.where(low, k, mask_feats_k(segk, HD).astype(bf)),
        jnp.where(low, mask_feats_k(segk, 0).astype(bf), k),
    ]


def fwd_kernel(*refs, tq, parts):
    q_ref, seg_ref = refs[0], refs[1]
    k_refs, v_refs = refs[2 : 2 + parts], refs[2 + parts : 2 + 2 * parts]
    o_ref, lse_ref = refs[2 + 2 * parts :]
    n = q_ref.shape[0]
    v = jnp.concatenate([r[...] for r in v_refs])
    seg = seg_ref[...]
    ks = [jnp.concatenate(x) for x in zip(*[both_masks(r[...], seg) for r in k_refs])]
    for t in range(n // tq):
        rows = pl.ds(t * tq, tq)
        q = q_ref[rows, :] * jnp.asarray(0.125, bf)
        lq = lanes(q.shape) < HD
        segq = seg_ref[rows, :]
        outs, lses = [], []
        for h in range(2):
            feats = mask_feats_q(segq, HD if h == 0 else 0).astype(bf)
            qq = jnp.where(lq, q, feats) if h == 0 else jnp.where(lq, feats, q)
            s = nt(qq, ks[h])
            m = jnp.max(s, axis=-1, keepdims=True)
            p = jnp.exp(s - m)
            l = jnp.sum(p, axis=-1, keepdims=True)
            o = nn(p.astype(bf), v)
            outs.append(o / l)
            lses.append(m + jnp.log(l))
        o_ref[rows, :] = jnp.where(lq, outs[0], outs[1]).astype(bf)
        lse_ref[rows, :] = jnp.where(
            lq, jnp.broadcast_to(lses[0], q.shape), jnp.broadcast_to(lses[1], q.shape)
        )


def specs(n, d, first=0):
    col = pl.BlockSpec((n, 2 * HD), lambda h: (0, h + first))
    val = pl.BlockSpec((n, 2 * HD), lambda h: (0, h + first + d // (2 * HD)))
    seg = pl.BlockSpec((n, 1), lambda h: (0, 0))
    return col, val, seg


def attn_fwd(q, blocks, seg, tq=256):
    n, d = q.shape
    parts = len(blocks)
    col, val, one = specs(n, d)
    return pl.pallas_call(
        functools.partial(fwd_kernel, tq=min(tq, n), parts=parts),
        grid=(d // (2 * HD),),
        in_specs=[col, one] + [col] * parts + [val] * parts,
        out_specs=[col, col],
        out_shape=[jax.ShapeDtypeStruct((n, d), bf), jax.ShapeDtypeStruct((n, d), f32)],
        cost_estimate=pl.CostEstimate(
            flops=16 * n * n * parts * d, bytes_accessed=n * d * (8 + 4 * parts), transcendentals=0
        ),
        name="attn_fwd",
    )(q, seg[:, None], *blocks, *blocks)


def bwd_kernel(*refs, tq, parts):
    q_ref, do_ref, o_ref, lse_ref, seg_ref = refs[:5]
    k_refs, v_refs = refs[5 : 5 + parts], refs[5 + parts : 5 + 2 * parts]
    dq_ref = refs[5 + 2 * parts]
    dkv_refs = refs[6 + 2 * parts : 6 + 3 * parts]
    acc_ref = refs[6 + 3 * parts]
    n = q_ref.shape[0]
    seg = seg_ref[...]
    group = min(2, parts)
    for c in range(0, parts, group):
        k = jnp.concatenate([r[...] for r in k_refs[c : c + group]])
        v = jnp.concatenate([r[...] for r in v_refs[c : c + group]])
        ks = both_masks(k, jnp.concatenate([seg] * group))
        lk = lanes(k.shape) < HD
        z = jnp.zeros_like(k)
        km = [jnp.where(lk, k, z), jnp.where(lk, z, k)]
        dk = jnp.zeros(k.shape, f32)
        dv = jnp.zeros(k.shape, f32)
        for t in range(n // tq):
            rows = pl.ds(t * tq, tq)
            q = q_ref[rows, :] * jnp.asarray(0.125, bf)
            do = do_ref[rows, :]
            lq = lanes(q.shape) < HD
            zq = jnp.zeros_like(q)
            segq = seg_ref[rows, :]
            lse = lse_ref[rows, :]
            prod = do.astype(f32) * o_ref[rows, :].astype(f32)
            dqs = None
            for h in range(2):
                own = lq if h == 0 else ~lq
                qq = jnp.where(own, q, mask_feats_q(segq, HD if h == 0 else 0).astype(bf))
                qm = jnp.where(own, q, zq)
                dom = jnp.where(own, do, zq)
                dd = jnp.sum(jnp.where(own, prod, 0.0), axis=-1, keepdims=True)
                ls = lse[:, :1] if h == 0 else lse[:, HD : HD + 1]
                p = jnp.exp(nt(qq, ks[h]) - ls)
                ds = (p * (nt(dom, v) - dd)).astype(bf)
                dv = dv + tn(p.astype(bf), dom)
                dk = dk + tn(ds, qm)
                x = nn(ds, km[h])
                dqs = x if dqs is None else dqs + x
            if c == 0:
                acc_ref[rows, :] = dqs
            else:
                acc_ref[rows, :] += dqs
        for i in range(group):
            dkv_refs[c + i][0] = dk[i * n : (i + 1) * n].astype(bf)
            dkv_refs[c + i][1] = dv[i * n : (i + 1) * n].astype(bf)
    dq_ref[...] = (acc_ref[...] * 0.125).astype(bf)


def attn_bwd(q, blocks, do, o, lse, seg, first, count, tq=256):
    n, d = q.shape
    parts = len(blocks)
    wide = count * 2 * HD
    col, val, one = specs(n, d, first)
    out = pl.BlockSpec((n, 2 * HD), lambda h: (0, h))
    pair = pl.BlockSpec((2, n, 2 * HD), lambda h: (0, 0, h))
    return pl.pallas_call(
        functools.partial(bwd_kernel, tq=min(tq, n), parts=parts),
        grid=(count,),
        in_specs=[col, col, col, col, one] + [col] * parts + [val] * parts,
        out_specs=[out] + [pair] * parts,
        out_shape=[jax.ShapeDtypeStruct((n, wide), bf)] + [jax.ShapeDtypeStruct((2, n, wide), bf)] * parts,
        scratch_shapes=[pltpu.VMEM((n, 2 * HD), f32)],
        cost_estimate=pl.CostEstimate(
            flops=40 * n * n * parts * wide, bytes_accessed=n * wide * (12 + 8 * parts), transcendentals=0
        ),
        name="attn_bwd",
    )(q, do, o, lse, seg[:, None], *blocks, *blocks)


def normed(value, gain, shift):
    center = value - jnp.mean(value, axis=-1, keepdims=True)
    spread = jnp.mean(center * center, axis=-1, keepdims=True)
    return center * lax.rsqrt(spread + 1e-06) * gain + shift


def gelu_tanh(value):
    return jax.nn.gelu(value, approximate=True)


def swap(x, flip):
    parts = lax.axis_size("band")
    return lax.ppermute(x, "band", [(i, i ^ flip) for i in range(parts)])


def gather_relative(x):
    return spread([x], lax.axis_size("band") // 2)


def spread(blocks, flip):
    while flip >= 1:
        blocks = blocks + [swap(block, flip) for block in blocks]
        flip //= 2
    return blocks


def tie(first, second):
    return lax.optimization_barrier((first, second))


def fold(blocks, flip):
    half = len(blocks) // 2
    return [
        (near.astype(f32) + swap(far, flip).astype(f32)).astype(bf)
        for near, far in zip(blocks[:half], blocks[half:])
    ]


def reduce_relative(blocks, flip=1):
    while len(blocks) > 1:
        blocks = fold(blocks, flip)
        flip *= 2
    return blocks[0]


def gather_vectors(shards):
    packed = jnp.concatenate(shards)
    whole = lax.all_gather(packed, "band", axis=0, tiled=False)
    out, at = [], 0
    for shard in shards:
        out.append(whole[:, at : at + shard.shape[0]].reshape(-1).astype(f32))
        at += shard.shape[0]
    return out


def relative_rows(array):
    me = lax.axis_index("band")
    order = [0]
    flip = lax.axis_size("band") // 2
    while flip >= 1:
        order = order + [i ^ flip for i in order]
        flip //= 2
    return [lax.dynamic_index_in_dim(array, me ^ i, 0, keepdims=False) for i in order]


def reduce_last(matrix, grads, shards):
    parts, columns = lax.axis_size("band"), matrix.shape[1]
    packed = jnp.concatenate([g.reshape(parts, -1) for g in grads], axis=1).astype(bf)
    rows = -(-packed.shape[1] // (16 * columns)) * 16
    packed = jnp.pad(packed, ((0, 0), (0, rows * columns - packed.shape[1])))
    mine = reduce_relative(relative_rows(matrix.astype(bf).reshape(parts, -1, columns)))
    extra = reduce_relative(relative_rows(packed.reshape(parts, rows, columns)))
    total = finish(mine, 1)
    vector = sum_small(extra).reshape(-1)
    out, at = [], 0
    for shard in shards:
        out.append(vector[at : at + shard.shape[0]])
        at += shard.shape[0]
    return total, out


def gather_matrix(shard):
    return lax.all_gather(shard, "band", axis=0, tiled=True)


def reduce_band(grad):
    blocks = grad.reshape(lax.axis_size("band"), -1, grad.shape[1])
    return reduce_relative(relative_rows(blocks))


def trade(x, flip):
    size = lax.axis_size("dp")
    return lax.ppermute(x, "dp", [(i, i ^ flip) for i in range(size)])


def halve(x, flip):
    bit = lax.rem(lax.axis_index("dp") // flip, 2)
    halves = x.reshape(2, -1, x.shape[1])
    near = lax.dynamic_index_in_dim(halves, bit, 0, keepdims=False)
    far = lax.dynamic_index_in_dim(halves, 1 - bit, 0, keepdims=False)
    return (near.astype(f32) + trade(far, flip).astype(f32)).astype(bf)


def join(x, flip):
    bit = lax.rem(lax.axis_index("dp") // flip, 2)
    other = trade(x, flip)
    return jnp.where(bit == 0, jnp.concatenate([x, other]), jnp.concatenate([other, x]))


def finish(x, flip):
    size = lax.axis_size("dp")
    while flip < size:
        x = halve(x, flip)
        flip *= 2
    while flip > 1:
        flip //= 2
        x = join(x, flip)
    return x.astype(f32)


def sum_small(x):
    flip = 1
    while flip < lax.axis_size("dp"):
        x = (x.astype(f32) + trade(x, flip).astype(f32)).astype(bf)
        flip *= 2
    return x.astype(f32)


def layer(inputs, segments, cotangent, ln1_gain, ln1_bias, w_qkv, b_qv, w_out, b_out, ln2_gain, ln2_bias, w_up, b_up, w_down, b_down):
    micro, tokens, width = inputs.shape[0], inputs.shape[2], inputs.shape[3]
    vectors = (ln1_gain, ln1_bias, b_qv, b_out, ln2_gain, ln2_bias, b_up, b_down)
    gain_one, shift_one, bias_qv, bias_out, gain_two, shift_two, bias_up, bias_down = gather_vectors(vectors)
    w_proj = gather_matrix(w_qkv)

    value = inputs.reshape(micro * tokens, width).astype(f32)
    seg = segments.reshape(micro, tokens)
    normed_in, pull_one = jax.vjp(normed, value, gain_one, shift_one)
    normed_low = normed_in.astype(bf)
    projected = nn(normed_low, w_proj)
    query = (projected[:, :width] + bias_qv[:width]).astype(bf)
    pairs = jnp.concatenate(
        [projected[:, width : 2 * width], projected[:, 2 * width :] + bias_qv[width:]], axis=1
    ).astype(bf)

    gathered = [gather_relative(pairs[:tokens])]
    far = lax.axis_size("band") // 2
    started = []
    for m in range(1, micro):
        own = pairs[m * tokens : (m + 1) * tokens]
        started.append([own, swap(own, far)])
    gathered[0], (w_out, w_up, w_down) = tie(gathered[0], (w_out, w_up, w_down))
    w_mix = gather_matrix(w_out)
    w_rise = gather_matrix(w_up)
    w_fall = gather_matrix(w_down)

    saved, mixes = [], []
    for m in range(micro):
        rows = slice(m * tokens, (m + 1) * tokens)
        if m > 0:
            blocks, mixes[m - 1] = tie(started[m - 1], mixes[m - 1])
            gathered.append(spread(blocks, far // 2))
        mix, log_total = attn_fwd(query[rows], gathered[m], seg[m])
        mixes.append(mix)
        saved.append((query[rows], gathered[m], mix, log_total, seg[m]))
    mixed = jnp.concatenate(mixes)

    hidden = value + (nn(mixed, w_mix) + bias_out)
    normed_mid, pull_two = jax.vjp(normed, hidden, gain_two, shift_two)
    mid_low = normed_mid.astype(bf)
    upward = nn(mid_low, w_rise) + bias_up
    active, pull_gelu = jax.vjp(gelu_tanh, upward)
    active_low = active.astype(bf)
    output = (hidden + (nn(active_low, w_fall) + bias_down)).astype(bf)

    real = (seg.reshape(-1, 1) != 0).astype(f32)
    grad_y = cotangent.reshape(micro * tokens, width).astype(f32) * real
    grad_m = grad_y.astype(bf)
    grad_w_fall = tn(active_low, grad_m)
    grad_b_fall = jnp.sum(grad_m.astype(f32), axis=0)
    low_fall, grad_m = tie(grad_w_fall.astype(bf), grad_m)
    grad_up = pull_gelu(nt(grad_m, w_fall))[0].astype(bf)
    grad_w_rise = tn(mid_low, grad_up)
    grad_b_rise = jnp.sum(grad_up.astype(f32), axis=0)
    grad_mid, grad_gain_two, grad_shift_two = pull_two(nt(grad_up, w_rise))
    grad_hidden = grad_y + grad_mid
    grad_a = grad_hidden.astype(bf)
    grad_w_mix = tn(mixed, grad_a)
    grad_b_mix = jnp.sum(grad_a.astype(f32), axis=0)
    grad_mixed = nt(grad_a, w_mix).astype(bf)

    grad_mixed, *rest = lax.optimization_barrier((grad_mixed, grad_w_rise.astype(bf), grad_w_mix.astype(bf)))
    large = [low_fall, *rest]
    large = [reduce_band(grad) for grad in large]

    count = width // (4 * HD)
    calls = [(m, first) for m in range(micro) for first in range(0, 2 * count, count)]
    halves, grads_q = [], []
    for i, (m, first) in enumerate(calls):
        q, blocks, mix, log_total, seg_q = saved[m]
        grad_out = grad_mixed[m * tokens : (m + 1) * tokens]
        if i >= 2:
            halves[i - 2], grad_out = tie(halves[i - 2], grad_out)
        if i in (1, 2):
            large[i - 1], grad_out = tie(large[i - 1], grad_out)
        if i == 3:
            (large[2], halved), grad_out = tie((large[2], halve(large[0], 1)), grad_out)
        grad_q, *grad_blocks = attn_bwd(q, blocks, grad_out, mix, log_total, seg_q, first, count)
        halves.append(fold(grad_blocks, 1))
        grads_q.append(grad_q)
    pairs = []
    for half in halves:
        pairs.append(reduce_relative(half, 2))
    pairs, grads_q = tie(pairs, grads_q)
    wide = [finish(halved, 2), finish(large[1], 1), finish(large[2], 1)]
    grad_qkv = jnp.concatenate(
        [
            jnp.concatenate(
                [grads_q[i], grads_q[i + 1], pairs[i][0], pairs[i + 1][0], pairs[i][1], pairs[i + 1][1]], axis=1
            )
            for i in range(0, 2 * micro, 2)
        ]
    )
    grad_qkv = lax.optimization_barrier(grad_qkv)
    grad_w_proj = tn(normed_low, grad_qkv)
    sums = jnp.sum(grad_qkv.astype(f32), axis=0)
    grad_b_proj = jnp.concatenate([sums[:width], sums[2 * width :]])
    grad_norm_in, grad_gain_one, grad_shift_one = pull_one(nt(grad_qkv, w_proj))
    input_grad = (grad_hidden + grad_norm_in).astype(bf)

    last, small = reduce_last(
        grad_w_proj,
        (grad_gain_one, grad_shift_one, grad_b_proj, grad_b_mix, grad_gain_two, grad_shift_two, grad_b_rise, grad_b_fall),
        vectors,
    )
    return (
        output.reshape(inputs.shape),
        input_grad.reshape(inputs.shape),
        small[0],
        small[1],
        last,
        small[2],
        wide[2],
        small[3],
        small[4],
        small[5],
        wide[1],
        small[6],
        wide[0],
        small[7],
    )


def solution(mesh):
    split = P(None, "dp", "band", None)
    rows, vector = P("band", None), P("band")
    weights = (vector, vector, rows, vector, rows, vector, vector, vector, rows, vector, rows, vector)
    return jax.shard_map(
        layer,
        mesh=mesh,
        in_specs=(split, P(None, "dp", "band"), split) + weights,
        out_specs=(split, split) + weights,
        check_vma=False,
    )
```

```python
import functools

import jax
import jax.numpy as jnp
from jax import lax
from jax.sharding import PartitionSpec as P
from jax.experimental import pallas as pl
from jax.experimental.pallas import tpu as pltpu
bf=jnp.bfloat16; f32=jnp.float32
HD=64


def nt(a,b): return lax.dot_general(a,b,(((1,),(1,)),((),())),preferred_element_type=f32)


def nn(a,b): return lax.dot_general(a,b,(((1,),(0,)),((),())),preferred_element_type=f32)


def tn(a,b): return lax.dot_general(a,b,(((0,),(0,)),((),())),preferred_element_type=f32)


def lanes(shape): return lax.broadcasted_iota(jnp.int32,shape,1)


NEG=-1e30


def mask_feats_q(seg, base):
    l=lanes((seg.shape[0],2*HD))
    return (l==seg+base).astype(f32)


def mask_feats_k(seg, base):
    l=lanes((seg.shape[0],2*HD))
    inr=(l>=base)&(l<base+8)
    return jnp.where(inr&(l!=seg+base),NEG,0.0)


def both_masks(k, segk):
    low = lanes(k.shape) < HD
    return [
        jnp.where(low, k, mask_feats_k(segk, HD).astype(bf)),
        jnp.where(low, mask_feats_k(segk, 0).astype(bf), k),
    ]


def fwd_kernel(*refs, tq, parts):
    q_ref, seg_ref = refs[0], refs[1]
    k_refs, v_refs = refs[2 : 2 + parts], refs[2 + parts : 2 + 2 * parts]
    o_ref, lse_ref = refs[2 + 2 * parts :]
    n = q_ref.shape[0]
    v = jnp.concatenate([r[...] for r in v_refs])
    seg = seg_ref[...]
    ks = [jnp.concatenate(x) for x in zip(*[both_masks(r[...], seg) for r in k_refs])]
    for t in range(n // tq):
        rows = pl.ds(t * tq, tq)
        q = q_ref[rows, :] * jnp.asarray(0.125, bf)
        lq = lanes(q.shape) < HD
        segq = seg_ref[rows, :]
        outs, lses = [], []
        for h in range(2):
            feats = mask_feats_q(segq, HD if h == 0 else 0).astype(bf)
            qq = jnp.where(lq, q, feats) if h == 0 else jnp.where(lq, feats, q)
            s = nt(qq, ks[h])
            m = jnp.max(s, axis=-1, keepdims=True)
            p = jnp.exp(s - m)
            l = jnp.sum(p, axis=-1, keepdims=True)
            o = nn(p.astype(bf), v)
            outs.append(o / l)
            lses.append(m + jnp.log(l))
        o_ref[rows, :] = jnp.where(lq, outs[0], outs[1]).astype(bf)
        lse_ref[rows, :] = jnp.where(
            lq, jnp.broadcast_to(lses[0], q.shape), jnp.broadcast_to(lses[1], q.shape)
        )


def specs(n, d, first=0):
    col = pl.BlockSpec((n, 2 * HD), lambda h: (0, h + first))
    val = pl.BlockSpec((n, 2 * HD), lambda h: (0, h + first + d // (2 * HD)))
    seg = pl.BlockSpec((n, 1), lambda h: (0, 0))
    return col, val, seg


def attn_fwd(q, blocks, seg, tq=256):
    n, d = q.shape
    parts = len(blocks)
    col, val, one = specs(n, d)
    return pl.pallas_call(
        functools.partial(fwd_kernel, tq=min(tq, n), parts=parts),
        grid=(d // (2 * HD),),
        in_specs=[col, one] + [col] * parts + [val] * parts,
        out_specs=[col, col],
        out_shape=[jax.ShapeDtypeStruct((n, d), bf), jax.ShapeDtypeStruct((n, d), f32)],
        cost_estimate=pl.CostEstimate(
            flops=16 * n * n * parts * d, bytes_accessed=n * d * (8 + 4 * parts), transcendentals=0
        ),
        name="attn_fwd",
    )(q, seg[:, None], *blocks, *blocks)


def bwd_kernel(*refs, tq, parts):
    q_ref, do_ref, o_ref, lse_ref, seg_ref = refs[:5]
    k_refs, v_refs = refs[5 : 5 + parts], refs[5 + parts : 5 + 2 * parts]
    dq_ref = refs[5 + 2 * parts]
    dkv_refs = refs[6 + 2 * parts : 6 + 3 * parts]
    acc_ref = refs[6 + 3 * parts]
    n = q_ref.shape[0]
    seg = seg_ref[...]
    group = min(2, parts)
    for c in range(0, parts, group):
        k = jnp.concatenate([r[...] for r in k_refs[c : c + group]])
        v = jnp.concatenate([r[...] for r in v_refs[c : c + group]])
        ks = both_masks(k, jnp.concatenate([seg] * group))
        lk = lanes(k.shape) < HD
        z = jnp.zeros_like(k)
        km = [jnp.where(lk, k, z), jnp.where(lk, z, k)]
        dk = jnp.zeros(k.shape, f32)
        dv = jnp.zeros(k.shape, f32)
        for t in range(n // tq):
            rows = pl.ds(t * tq, tq)
            q = q_ref[rows, :] * jnp.asarray(0.125, bf)
            do = do_ref[rows, :]
            lq = lanes(q.shape) < HD
            zq = jnp.zeros_like(q)
            segq = seg_ref[rows, :]
            lse = lse_ref[rows, :]
            prod = do.astype(f32) * o_ref[rows, :].astype(f32)
            dqs = None
            for h in range(2):
                own = lq if h == 0 else ~lq
                qq = jnp.where(own, q, mask_feats_q(segq, HD if h == 0 else 0).astype(bf))
                qm = jnp.where(own, q, zq)
                dom = jnp.where(own, do, zq)
                dd = jnp.sum(jnp.where(own, prod, 0.0), axis=-1, keepdims=True)
                ls = lse[:, :1] if h == 0 else lse[:, HD : HD + 1]
                p = jnp.exp(nt(qq, ks[h]) - ls)
                ds = (p * (nt(dom, v) - dd)).astype(bf)
                dv = dv + tn(p.astype(bf), dom)
                dk = dk + tn(ds, qm)
                x = nn(ds, km[h])
                dqs = x if dqs is None else dqs + x
            if c == 0:
                acc_ref[rows, :] = dqs
            else:
                acc_ref[rows, :] += dqs
        for i in range(group):
            dkv_refs[c + i][0] = dk[i * n : (i + 1) * n].astype(bf)
            dkv_refs[c + i][1] = dv[i * n : (i + 1) * n].astype(bf)
    dq_ref[...] = (acc_ref[...] * 0.125).astype(bf)


def attn_bwd(q, blocks, do, o, lse, seg, first, count, tq=256):
    n, d = q.shape
    parts = len(blocks)
    wide = count * 2 * HD
    col, val, one = specs(n, d, first)
    out = pl.BlockSpec((n, 2 * HD), lambda h: (0, h))
    pair = pl.BlockSpec((2, n, 2 * HD), lambda h: (0, 0, h))
    return pl.pallas_call(
        functools.partial(bwd_kernel, tq=min(tq, n), parts=parts),
        grid=(count,),
        in_specs=[col, col, col, col, one] + [col] * parts + [val] * parts,
        out_specs=[out] + [pair] * parts,
        out_shape=[jax.ShapeDtypeStruct((n, wide), bf)] + [jax.ShapeDtypeStruct((2, n, wide), bf)] * parts,
        scratch_shapes=[pltpu.VMEM((n, 2 * HD), f32)],
        cost_estimate=pl.CostEstimate(
            flops=40 * n * n * parts * wide, bytes_accessed=n * wide * (12 + 8 * parts), transcendentals=0
        ),
        name="attn_bwd",
    )(q, do, o, lse, seg[:, None], *blocks, *blocks)


def normed(value, gain, shift):
    center = value - jnp.mean(value, axis=-1, keepdims=True)
    spread = jnp.mean(center * center, axis=-1, keepdims=True)
    return center * lax.rsqrt(spread + 1e-06) * gain + shift


def gelu_tanh(value):
    return jax.nn.gelu(value, approximate=True)


def swap(x, flip):
    parts = lax.axis_size("band")
    return lax.ppermute(x, "band", [(i, i ^ flip) for i in range(parts)])


def gather_relative(x):
    return spread([x], lax.axis_size("band") // 2)


def spread(blocks, flip):
    while flip >= 1:
        blocks = blocks + [swap(block, flip) for block in blocks]
        flip //= 2
    return blocks


def tie(first, second):
    return lax.optimization_barrier((first, second))


def fold(blocks, flip):
    half = len(blocks) // 2
    return [
        (near.astype(f32) + swap(far, flip).astype(f32)).astype(bf)
        for near, far in zip(blocks[:half], blocks[half:])
    ]


def reduce_relative(blocks, flip=1):
    while len(blocks) > 1:
        blocks = fold(blocks, flip)
        flip *= 2
    return blocks[0]


def gather_vectors(shards):
    packed = jnp.concatenate(shards)
    whole = lax.all_gather(packed, "band", axis=0, tiled=False)
    out, at = [], 0
    for shard in shards:
        out.append(whole[:, at : at + shard.shape[0]].reshape(-1).astype(f32))
        at += shard.shape[0]
    return out


def relative_rows(array):
    me = lax.axis_index("band")
    order = [0]
    flip = lax.axis_size("band") // 2
    while flip >= 1:
        order = order + [i ^ flip for i in order]
        flip //= 2
    return [lax.dynamic_index_in_dim(array, me ^ i, 0, keepdims=False) for i in order]


def reduce_last(matrix, grads, shards):
    parts, columns = lax.axis_size("band"), matrix.shape[1]
    packed = jnp.concatenate([g.reshape(parts, -1) for g in grads], axis=1).astype(bf)
    rows = -(-packed.shape[1] // (16 * columns)) * 16
    packed = jnp.pad(packed, ((0, 0), (0, rows * columns - packed.shape[1])))
    mine = reduce_relative(relative_rows(matrix.astype(bf).reshape(parts, -1, columns)))
    extra = reduce_relative(relative_rows(packed.reshape(parts, rows, columns)))
    total = finish(mine, 1)
    vector = sum_small(extra).reshape(-1)
    out, at = [], 0
    for shard in shards:
        out.append(vector[at : at + shard.shape[0]])
        at += shard.shape[0]
    return total, out


def gather_matrix(shard):
    return lax.all_gather(shard, "band", axis=0, tiled=True)


def reduce_core(grad):
    blocks = grad.reshape(lax.axis_size("band"), -1, grad.shape[1])
    return fold(relative_rows(blocks), 1)


def reduce_chip(blocks):
    return reduce_relative(blocks, 2)


def trade(x, flip):
    size = lax.axis_size("dp")
    return lax.ppermute(x, "dp", [(i, i ^ flip) for i in range(size)])


def halve(x, flip):
    bit = lax.rem(lax.axis_index("dp") // flip, 2)
    halves = x.reshape(2, -1, x.shape[1])
    near = lax.dynamic_index_in_dim(halves, bit, 0, keepdims=False)
    far = lax.dynamic_index_in_dim(halves, 1 - bit, 0, keepdims=False)
    return (near.astype(f32) + trade(far, flip).astype(f32)).astype(bf)


def join(x, flip):
    bit = lax.rem(lax.axis_index("dp") // flip, 2)
    other = trade(x, flip)
    return jnp.where(bit == 0, jnp.concatenate([x, other]), jnp.concatenate([other, x]))


def finish(x, flip):
    size = lax.axis_size("dp")
    while flip < size:
        x = halve(x, flip)
        flip *= 2
    while flip > 1:
        flip //= 2
        x = join(x, flip)
    return x.astype(f32)


def sum_small(x):
    flip = 1
    while flip < lax.axis_size("dp"):
        x = (x.astype(f32) + trade(x, flip).astype(f32)).astype(bf)
        flip *= 2
    return x.astype(f32)


def layer(inputs, segments, cotangent, ln1_gain, ln1_bias, w_qkv, b_qv, w_out, b_out, ln2_gain, ln2_bias, w_up, b_up, w_down, b_down):
    micro, tokens, width = inputs.shape[0], inputs.shape[2], inputs.shape[3]
    vectors = (ln1_gain, ln1_bias, b_qv, b_out, ln2_gain, ln2_bias, b_up, b_down)
    gain_one, shift_one, bias_qv, bias_out, gain_two, shift_two, bias_up, bias_down = gather_vectors(vectors)
    w_proj = gather_matrix(w_qkv)

    value = inputs.reshape(micro * tokens, width).astype(f32)
    seg = segments.reshape(micro, tokens)
    normed_in, pull_one = jax.vjp(normed, value, gain_one, shift_one)
    normed_low = normed_in.astype(bf)
    projected = nn(normed_low, w_proj)
    query = (projected[:, :width] + bias_qv[:width]).astype(bf)
    pairs = jnp.concatenate(
        [projected[:, width : 2 * width], projected[:, 2 * width :] + bias_qv[width:]], axis=1
    ).astype(bf)

    gathered = [gather_relative(pairs[:tokens])]
    far = lax.axis_size("band") // 2
    started = []
    for m in range(1, micro):
        own = pairs[m * tokens : (m + 1) * tokens]
        started.append([own, swap(own, far)])
    gathered[0], (w_out, w_up, w_down) = tie(gathered[0], (w_out, w_up, w_down))
    w_mix = gather_matrix(w_out)
    w_rise = gather_matrix(w_up)
    w_fall = gather_matrix(w_down)

    saved, mixes = [], []
    for m in range(micro):
        rows = slice(m * tokens, (m + 1) * tokens)
        if m > 0:
            blocks, mixes[m - 1] = tie(started[m - 1], mixes[m - 1])
            gathered.append(spread(blocks, far // 2))
        mix, log_total = attn_fwd(query[rows], gathered[m], seg[m])
        mixes.append(mix)
        saved.append((query[rows], gathered[m], mix, log_total, seg[m]))
    mixed = jnp.concatenate(mixes)

    hidden = value + (nn(mixed, w_mix) + bias_out)
    normed_mid, pull_two = jax.vjp(normed, hidden, gain_two, shift_two)
    mid_low = normed_mid.astype(bf)
    upward = nn(mid_low, w_rise) + bias_up
    active, pull_gelu = jax.vjp(gelu_tanh, upward)
    active_low = active.astype(bf)
    output = (hidden + (nn(active_low, w_fall) + bias_down)).astype(bf)

    real = (seg.reshape(-1, 1) != 0).astype(f32)
    grad_y = cotangent.reshape(micro * tokens, width).astype(f32) * real
    grad_m = grad_y.astype(bf)
    grad_w_fall = tn(active_low, grad_m)
    grad_b_fall = jnp.sum(grad_m.astype(f32), axis=0)
    low_fall, grad_m = tie(grad_w_fall.astype(bf), grad_m)
    fall = reduce_core(low_fall)
    grad_up = pull_gelu(nt(grad_m, w_fall))[0].astype(bf)
    fall, grad_up = tie(fall, grad_up)
    fall = reduce_chip(fall)
    grad_w_rise = tn(mid_low, grad_up)
    grad_b_rise = jnp.sum(grad_up.astype(f32), axis=0)
    grad_mid, grad_gain_two, grad_shift_two = pull_two(nt(grad_up, w_rise))
    grad_hidden = grad_y + grad_mid
    grad_a = grad_hidden.astype(bf)
    grad_w_mix = tn(mixed, grad_a)
    grad_b_mix = jnp.sum(grad_a.astype(f32), axis=0)
    grad_mixed = nt(grad_a, w_mix).astype(bf)

    grad_mixed, *rest = lax.optimization_barrier((grad_mixed, grad_w_rise.astype(bf), grad_w_mix.astype(bf)))
    rise, out_grad = reduce_core(rest[0]), reduce_core(rest[1])

    count = width // (4 * HD)
    calls = [(m, first) for m in range(micro) for first in range(0, 2 * count, count)]
    halves, grads_q = [], []
    for i, (m, first) in enumerate(calls):
        q, blocks, mix, log_total, seg_q = saved[m]
        grad_out = grad_mixed[m * tokens : (m + 1) * tokens]
        if i >= 2:
            halves[i - 2], grad_out = tie(halves[i - 2], grad_out)
        if i == 1:
            (fall, rise, out_grad), grad_out = tie((fall, rise, out_grad), grad_out)
            rise, out_grad = reduce_chip(rise), reduce_chip(out_grad)
            fall = halve(fall, 1)
        if i == 3:
            (fall, rise, out_grad), grad_out = tie((fall, rise, out_grad), grad_out)
            rise = halve(rise, 1)
        grad_q, *grad_blocks = attn_bwd(q, blocks, grad_out, mix, log_total, seg_q, first, count)
        halves.append(fold(grad_blocks, 1))
        grads_q.append(grad_q)
    pairs = []
    for half in halves:
        pairs.append(reduce_relative(half, 2))
    pairs, grads_q = tie(pairs, grads_q)
    wide = [finish(fall, 2), finish(rise, 2), finish(out_grad, 1)]
    grad_qkv = jnp.concatenate(
        [
            jnp.concatenate(
                [grads_q[i], grads_q[i + 1], pairs[i][0], pairs[i + 1][0], pairs[i][1], pairs[i + 1][1]], axis=1
            )
            for i in range(0, 2 * micro, 2)
        ]
    )
    grad_qkv = lax.optimization_barrier(grad_qkv)
    grad_w_proj = tn(normed_low, grad_qkv)
    sums = jnp.sum(grad_qkv.astype(f32), axis=0)
    grad_b_proj = jnp.concatenate([sums[:width], sums[2 * width :]])
    grad_norm_in, grad_gain_one, grad_shift_one = pull_one(nt(grad_qkv, w_proj))
    input_grad = (grad_hidden + grad_norm_in).astype(bf)

    last, small = reduce_last(
        grad_w_proj,
        (grad_gain_one, grad_shift_one, grad_b_proj, grad_b_mix, grad_gain_two, grad_shift_two, grad_b_rise, grad_b_fall),
        vectors,
    )
    return (
        output.reshape(inputs.shape),
        input_grad.reshape(inputs.shape),
        small[0],
        small[1],
        last,
        small[2],
        wide[2],
        small[3],
        small[4],
        small[5],
        wide[1],
        small[6],
        wide[0],
        small[7],
    )


def solution(mesh):
    split = P(None, "dp", "band", None)
    rows, vector = P("band", None), P("band")
    weights = (vector, vector, rows, vector, rows, vector, vector, vector, rows, vector, rows, vector)
    return jax.shard_map(
        layer,
        mesh=mesh,
        in_specs=(split, P(None, "dp", "band"), split) + weights,
        out_specs=(split, split) + weights,
        check_vma=False,
    )
```

```python
import functools

import jax
import jax.numpy as jnp
from jax import lax
from jax.sharding import PartitionSpec as P
from jax.experimental import pallas as pl
from jax.experimental.pallas import tpu as pltpu
bf=jnp.bfloat16; f32=jnp.float32
HD=64


def nt(a,b): return lax.dot_general(a,b,(((1,),(1,)),((),())),preferred_element_type=f32)


def nn(a,b): return lax.dot_general(a,b,(((1,),(0,)),((),())),preferred_element_type=f32)


def tn(a,b): return lax.dot_general(a,b,(((0,),(0,)),((),())),preferred_element_type=f32)


def lanes(shape): return lax.broadcasted_iota(jnp.int32,shape,1)


NEG=-1e30


def mask_feats_q(seg, base):
    l=lanes((seg.shape[0],2*HD))
    return (l==seg+base).astype(f32)


def mask_feats_k(seg, base):
    l=lanes((seg.shape[0],2*HD))
    inr=(l>=base)&(l<base+8)
    return jnp.where(inr&(l!=seg+base),NEG,0.0)


def both_masks(k, segk):
    low = lanes(k.shape) < HD
    return [
        jnp.where(low, k, mask_feats_k(segk, HD).astype(bf)),
        jnp.where(low, mask_feats_k(segk, 0).astype(bf), k),
    ]


def fwd_kernel(*refs, tq, parts):
    q_ref, seg_ref = refs[0], refs[1]
    k_refs, v_refs = refs[2 : 2 + parts], refs[2 + parts : 2 + 2 * parts]
    o_ref, lse_ref = refs[2 + 2 * parts :]
    n = q_ref.shape[0]
    v = jnp.concatenate([r[...] for r in v_refs])
    seg = seg_ref[...]
    ks = [jnp.concatenate(x) for x in zip(*[both_masks(r[...], seg) for r in k_refs])]
    for t in range(n // tq):
        rows = pl.ds(t * tq, tq)
        q = q_ref[rows, :] * jnp.asarray(0.125, bf)
        lq = lanes(q.shape) < HD
        segq = seg_ref[rows, :]
        outs, lses = [], []
        for h in range(2):
            feats = mask_feats_q(segq, HD if h == 0 else 0).astype(bf)
            qq = jnp.where(lq, q, feats) if h == 0 else jnp.where(lq, feats, q)
            s = nt(qq, ks[h])
            m = jnp.max(s, axis=-1, keepdims=True)
            p = jnp.exp(s - m)
            l = jnp.sum(p, axis=-1, keepdims=True)
            o = nn(p.astype(bf), v)
            outs.append(o / l)
            lses.append(m + jnp.log(l))
        o_ref[rows, :] = jnp.where(lq, outs[0], outs[1]).astype(bf)
        lse_ref[rows, :] = jnp.where(
            lq, jnp.broadcast_to(lses[0], q.shape), jnp.broadcast_to(lses[1], q.shape)
        )


def specs(n, first, count):
    wide = pl.BlockSpec((n, 2 * HD), lambda h: (0, h + first))
    key = pl.BlockSpec((n, 2 * HD), lambda h: (0, h))
    val = pl.BlockSpec((n, 2 * HD), lambda h: (0, h + count))
    seg = pl.BlockSpec((n, 1), lambda h: (0, 0))
    return wide, key, val, seg


def attn_fwd(q, blocks, seg, first, count, tq=256):
    n = q.shape[0]
    parts, d = len(blocks), count * 2 * HD
    wide, key, val, one = specs(n, first, count)
    return pl.pallas_call(
        functools.partial(fwd_kernel, tq=min(tq, n), parts=parts),
        grid=(count,),
        in_specs=[wide, one] + [key] * parts + [val] * parts,
        out_specs=[key, key],
        out_shape=[jax.ShapeDtypeStruct((n, d), bf), jax.ShapeDtypeStruct((n, d), f32)],
        cost_estimate=pl.CostEstimate(
            flops=16 * n * n * parts * d, bytes_accessed=n * d * (8 + 4 * parts), transcendentals=0
        ),
        name="attn_fwd",
    )(q, seg[:, None], *blocks, *blocks)


def bwd_kernel(*refs, tq, parts):
    q_ref, do_ref, o_ref, lse_ref, seg_ref = refs[:5]
    k_refs, v_refs = refs[5 : 5 + parts], refs[5 + parts : 5 + 2 * parts]
    dq_ref = refs[5 + 2 * parts]
    dkv_refs = refs[6 + 2 * parts : 6 + 3 * parts]
    acc_ref = refs[6 + 3 * parts]
    n = q_ref.shape[0]
    seg = seg_ref[...]
    group = min(2, parts)
    for c in range(0, parts, group):
        k = jnp.concatenate([r[...] for r in k_refs[c : c + group]])
        v = jnp.concatenate([r[...] for r in v_refs[c : c + group]])
        ks = both_masks(k, jnp.concatenate([seg] * group))
        lk = lanes(k.shape) < HD
        z = jnp.zeros_like(k)
        km = [jnp.where(lk, k, z), jnp.where(lk, z, k)]
        dk = jnp.zeros(k.shape, f32)
        dv = jnp.zeros(k.shape, f32)
        for t in range(n // tq):
            rows = pl.ds(t * tq, tq)
            q = q_ref[rows, :] * jnp.asarray(0.125, bf)
            do = do_ref[rows, :]
            lq = lanes(q.shape) < HD
            zq = jnp.zeros_like(q)
            segq = seg_ref[rows, :]
            lse = lse_ref[rows, :]
            prod = do.astype(f32) * o_ref[rows, :].astype(f32)
            dqs = None
            for h in range(2):
                own = lq if h == 0 else ~lq
                qq = jnp.where(own, q, mask_feats_q(segq, HD if h == 0 else 0).astype(bf))
                qm = jnp.where(own, q, zq)
                dom = jnp.where(own, do, zq)
                dd = jnp.sum(jnp.where(own, prod, 0.0), axis=-1, keepdims=True)
                ls = lse[:, :1] if h == 0 else lse[:, HD : HD + 1]
                p = jnp.exp(nt(qq, ks[h]) - ls)
                ds = (p * (nt(dom, v) - dd)).astype(bf)
                dv = dv + tn(p.astype(bf), dom)
                dk = dk + tn(ds, qm)
                x = nn(ds, km[h])
                dqs = x if dqs is None else dqs + x
            if c == 0:
                acc_ref[rows, :] = dqs
            else:
                acc_ref[rows, :] += dqs
        for i in range(group):
            dkv_refs[c + i][0] = dk[i * n : (i + 1) * n].astype(bf)
            dkv_refs[c + i][1] = dv[i * n : (i + 1) * n].astype(bf)
    dq_ref[...] = (acc_ref[...] * 0.125).astype(bf)


def attn_bwd(q, blocks, do, o, lse, seg, first, count, tq=256):
    n = q.shape[0]
    parts, d = len(blocks), count * 2 * HD
    wide, key, val, one = specs(n, first, count)
    pair = pl.BlockSpec((2, n, 2 * HD), lambda h: (0, 0, h))
    return pl.pallas_call(
        functools.partial(bwd_kernel, tq=min(tq, n), parts=parts),
        grid=(count,),
        in_specs=[wide, wide, key, key, one] + [key] * parts + [val] * parts,
        out_specs=[key] + [pair] * parts,
        out_shape=[jax.ShapeDtypeStruct((n, d), bf)] + [jax.ShapeDtypeStruct((2, n, d), bf)] * parts,
        scratch_shapes=[pltpu.VMEM((n, 2 * HD), f32)],
        cost_estimate=pl.CostEstimate(
            flops=40 * n * n * parts * d, bytes_accessed=n * d * (12 + 8 * parts), transcendentals=0
        ),
        name="attn_bwd",
    )(q, do, o, lse, seg[:, None], *blocks, *blocks)


def normed(value, gain, shift):
    center = value - jnp.mean(value, axis=-1, keepdims=True)
    spread = jnp.mean(center * center, axis=-1, keepdims=True)
    return center * lax.rsqrt(spread + 1e-06) * gain + shift


def gelu_tanh(value):
    return jax.nn.gelu(value, approximate=True)


def swap(x, flip):
    parts = lax.axis_size("band")
    return lax.ppermute(x, "band", [(i, i ^ flip) for i in range(parts)])


def spread(blocks, flip):
    while flip >= 1:
        blocks = blocks + [swap(block, flip) for block in blocks]
        flip //= 2
    return blocks


def tie(first, second):
    return lax.optimization_barrier((first, second))


def fold(blocks, flip):
    half = len(blocks) // 2
    return [
        (near.astype(f32) + swap(far, flip).astype(f32)).astype(bf)
        for near, far in zip(blocks[:half], blocks[half:])
    ]


def reduce_relative(blocks, flip=1):
    while len(blocks) > 1:
        blocks = fold(blocks, flip)
        flip *= 2
    return blocks[0]


def gather_vectors(shards):
    packed = jnp.concatenate(shards)
    whole = lax.all_gather(packed, "band", axis=0, tiled=False)
    out, at = [], 0
    for shard in shards:
        out.append(whole[:, at : at + shard.shape[0]].reshape(-1).astype(f32))
        at += shard.shape[0]
    return out


def relative_rows(array):
    me = lax.axis_index("band")
    order = [0]
    flip = lax.axis_size("band") // 2
    while flip >= 1:
        order = order + [i ^ flip for i in order]
        flip //= 2
    return [lax.dynamic_index_in_dim(array, me ^ i, 0, keepdims=False) for i in order]


def reduce_last(matrix, grads, shards):
    parts, columns = lax.axis_size("band"), matrix.shape[1]
    packed = jnp.concatenate([g.reshape(parts, -1) for g in grads], axis=1).astype(bf)
    rows = -(-packed.shape[1] // (16 * columns)) * 16
    packed = jnp.pad(packed, ((0, 0), (0, rows * columns - packed.shape[1])))
    mine = reduce_chip(reduce_core(matrix.astype(bf)))
    extra = reduce_relative(relative_rows(packed.reshape(parts, rows, columns)))
    vector = sum_small(extra).reshape(-1)
    total = finish(mine, 1)
    out, at = [], 0
    for shard in shards:
        out.append(vector[at : at + shard.shape[0]])
        at += shard.shape[0]
    return total, out


def gather_matrix(shard):
    return lax.all_gather(shard, "band", axis=0, tiled=True)


def reduce_core(grad):
    blocks = grad.reshape(lax.axis_size("band"), -1, grad.shape[1])
    return fold(relative_rows(blocks), 1)


def reduce_chip(blocks):
    return reduce_relative(blocks, 2)


def trade(x, flip):
    size = lax.axis_size("dp")
    return lax.ppermute(x, "dp", [(i, i ^ flip) for i in range(size)])


def halve(x, flip):
    bit = lax.rem(lax.axis_index("dp") // flip, 2)
    halves = x.reshape(2, -1, x.shape[1])
    near = lax.dynamic_index_in_dim(halves, bit, 0, keepdims=False)
    far = lax.dynamic_index_in_dim(halves, 1 - bit, 0, keepdims=False)
    return (near.astype(f32) + trade(far, flip).astype(f32)).astype(bf)


def join(x, flip):
    bit = lax.rem(lax.axis_index("dp") // flip, 2)
    other = trade(x, flip)
    return jnp.where(bit == 0, jnp.concatenate([x, other]), jnp.concatenate([other, x]))


def finish(x, flip):
    size = lax.axis_size("dp")
    while flip < size:
        x = halve(x, flip)
        flip *= 2
    while flip > 1:
        flip //= 2
        x = join(x, flip)
    return x.astype(f32)


def sum_small(x):
    flip = 1
    while flip < lax.axis_size("dp"):
        x = (x.astype(f32) + trade(x, flip).astype(f32)).astype(bf)
        flip *= 2
    return x.astype(f32)


def layer(inputs, segments, cotangent, ln1_gain, ln1_bias, w_qkv, b_qv, w_out, b_out, ln2_gain, ln2_bias, w_up, b_up, w_down, b_down):
    micro, tokens, width = inputs.shape[0], inputs.shape[2], inputs.shape[3]
    parts = lax.axis_size("band")
    vectors = (ln1_gain, ln1_bias, b_qv, b_out, ln2_gain, ln2_bias, b_up, b_down)
    gain_one, shift_one, bias_qv, bias_out, gain_two, shift_two, bias_up, bias_down = gather_vectors(vectors)
    w_proj = gather_matrix(w_qkv)

    value = inputs.reshape(micro * tokens, width).astype(f32)
    seg = segments.reshape(micro, tokens)
    normed_in, pull_one = jax.vjp(normed, value, gain_one, shift_one)
    normed_low = normed_in.astype(bf)
    projected = nn(normed_low, w_proj)
    query = (projected[:, :width] + bias_qv[:width]).astype(bf)
    keys = projected[:, width : 2 * width].astype(bf)
    values = (projected[:, 2 * width :] + bias_qv[width:]).astype(bf)

    count = width // (4 * HD)
    half = width // 2
    far = parts // 2
    units = [(m, first) for m in range(micro) for first in (0, count)]
    started = []
    for i, (m, first) in enumerate(units):
        rows, cols = slice(m * tokens, (m + 1) * tokens), slice(first * 2 * HD, first * 2 * HD + half)
        own = jnp.concatenate([keys[rows, cols], values[rows, cols]], axis=1)
        if i > 0:
            started[i - 1], own = tie(started[i - 1], own)
        started.append(own)
    for i, own in enumerate(started):
        started[i] = [own, swap(own, far)]

    saved, mixes = [], []
    for i, (m, first) in enumerate(units):
        blocks = started[i]
        if i > 0:
            blocks, mixes[i - 1] = tie(blocks, mixes[i - 1])
        blocks = spread(blocks, far // 2)
        if i == 0:
            blocks, (w_out, w_up, w_down) = tie(blocks, (w_out, w_up, w_down))
            w_mix = gather_matrix(w_out)
            w_rise = gather_matrix(w_up)
            w_fall = gather_matrix(w_down)
        q = query[m * tokens : (m + 1) * tokens]
        mix, log_total = attn_fwd(q, blocks, seg[m], first, count)
        mixes.append(mix)
        saved.append((q, blocks, mix, log_total, seg[m]))
    mixed = jnp.concatenate(
        [jnp.concatenate(mixes[i : i + 2], axis=1) for i in range(0, 2 * micro, 2)]
    )

    hidden = value + (nn(mixed, w_mix) + bias_out)
    normed_mid, pull_two = jax.vjp(normed, hidden, gain_two, shift_two)
    mid_low = normed_mid.astype(bf)
    upward = nn(mid_low, w_rise) + bias_up
    active, pull_gelu = jax.vjp(gelu_tanh, upward)
    active_low = active.astype(bf)

    real = (seg.reshape(-1, 1) != 0).astype(f32)
    grad_y = cotangent.reshape(micro * tokens, width).astype(f32) * real
    grad_m = grad_y.astype(bf)
    grad_w_fall = tn(active_low, grad_m)
    grad_b_fall = jnp.sum(grad_m.astype(f32), axis=0)
    low_fall, grad_m = tie(grad_w_fall.astype(bf), grad_m)
    fall = reduce_core(low_fall)
    grad_up = pull_gelu(nt(grad_m, w_fall))[0].astype(bf)
    fall, grad_up = tie(fall, grad_up)
    fall = reduce_chip(fall)
    grad_w_rise = tn(mid_low, grad_up)
    grad_mid, grad_gain_two, grad_shift_two = pull_two(nt(grad_up, w_rise))
    grad_hidden = grad_y + grad_mid
    grad_a = grad_hidden.astype(bf)
    grad_w_mix = tn(mixed, grad_a)
    grad_b_mix = jnp.sum(grad_a.astype(f32), axis=0)
    grad_mixed = nt(grad_a, w_mix).astype(bf)

    grad_mixed, *rest = lax.optimization_barrier((grad_mixed, grad_w_rise.astype(bf), grad_w_mix.astype(bf)))
    rise, out_grad = reduce_core(rest[0]), reduce_core(rest[1])

    halves, grads_q = [], []
    for i, (m, first) in enumerate(units):
        q, blocks, mix, log_total, seg_q = saved[i]
        grad_out = grad_mixed[m * tokens : (m + 1) * tokens]
        if i >= 2:
            halves[i - 2], grad_out = tie(halves[i - 2], grad_out)
        if i == 1:
            (fall, rise, out_grad), grad_out = tie((fall, rise, out_grad), grad_out)
            rise, out_grad = reduce_chip(rise), reduce_chip(out_grad)
            fall = halve(fall, 1)
        if i == 3:
            (fall, rise, out_grad), grad_out = tie((fall, rise, out_grad), grad_out)
            rise = halve(rise, 1)
        grad_q, *grad_blocks = attn_bwd(q, blocks, grad_out, mix, log_total, seg_q, first, count)
        halves.append(fold(grad_blocks, 1))
        grads_q.append(grad_q)
    halves[-1], (active_low, grad_up) = tie(halves[-1], (active_low, grad_up))
    output = (hidden + (nn(active_low, w_fall) + bias_down)).astype(bf)
    grad_b_rise = jnp.sum(grad_up.astype(f32), axis=0)
    pairs = []
    for half in halves:
        pairs.append(reduce_relative(half, 2))
    pairs, grads_q = tie(pairs, grads_q)
    grad_qkv = jnp.concatenate(
        [
            jnp.concatenate(
                [grads_q[i], grads_q[i + 1], pairs[i][0], pairs[i + 1][0], pairs[i][1], pairs[i + 1][1]], axis=1
            )
            for i in range(0, 2 * micro, 2)
        ]
    )
    (fall, rise, out_grad), grad_qkv = tie((fall, rise, out_grad), grad_qkv)
    wide = [finish(fall, 2), finish(rise, 2), finish(out_grad, 1)]
    grad_w_proj = tn(normed_low, grad_qkv)
    sums = jnp.sum(grad_qkv.astype(f32), axis=0)
    grad_b_proj = jnp.concatenate([sums[:width], sums[2 * width :]])
    grad_norm_in, grad_gain_one, grad_shift_one = pull_one(nt(grad_qkv, w_proj))
    input_grad = (grad_hidden + grad_norm_in).astype(bf)

    last, small = reduce_last(
        grad_w_proj,
        (grad_gain_one, grad_shift_one, grad_b_proj, grad_b_mix, grad_gain_two, grad_shift_two, grad_b_rise, grad_b_fall),
        vectors,
    )
    return (
        output.reshape(inputs.shape),
        input_grad.reshape(inputs.shape),
        small[0],
        small[1],
        last,
        small[2],
        wide[2],
        small[3],
        small[4],
        small[5],
        wide[1],
        small[6],
        wide[0],
        small[7],
    )


def solution(mesh):
    split = P(None, "dp", "band", None)
    rows, vector = P("band", None), P("band")
    weights = (vector, vector, rows, vector, rows, vector, vector, vector, rows, vector, rows, vector)
    return jax.shard_map(
        layer,
        mesh=mesh,
        in_specs=(split, P(None, "dp", "band"), split) + weights,
        out_specs=(split, split) + weights,
        check_vma=False,
    )
```

```python
import functools

import jax
import jax.numpy as jnp
from jax import lax
from jax.sharding import PartitionSpec as P
from jax.experimental import pallas as pl
from jax.experimental.pallas import tpu as pltpu
bf=jnp.bfloat16; f32=jnp.float32
HD=64


def nt(a,b): return lax.dot_general(a,b,(((1,),(1,)),((),())),preferred_element_type=f32)


def nn(a,b): return lax.dot_general(a,b,(((1,),(0,)),((),())),preferred_element_type=f32)


def tn(a,b): return lax.dot_general(a,b,(((0,),(0,)),((),())),preferred_element_type=f32)


def lanes(shape): return lax.broadcasted_iota(jnp.int32,shape,1)


NEG=-1e30


def mask_feats_q(seg, base):
    l=lanes((seg.shape[0],2*HD))
    return (l==seg+base).astype(f32)


def mask_feats_k(seg, base):
    l=lanes((seg.shape[0],2*HD))
    inr=(l>=base)&(l<base+8)
    return jnp.where(inr&(l!=seg+base),NEG,0.0)


def both_masks(k, segk):
    low = lanes(k.shape) < HD
    return [
        jnp.where(low, k, mask_feats_k(segk, HD).astype(bf)),
        jnp.where(low, mask_feats_k(segk, 0).astype(bf), k),
    ]


def fwd_kernel(*refs, tq, parts):
    q_ref, seg_ref = refs[0], refs[1]
    k_refs, v_refs = refs[2 : 2 + parts], refs[2 + parts : 2 + 2 * parts]
    o_ref, lse_ref = refs[2 + 2 * parts :]
    n = q_ref.shape[0]
    v = jnp.concatenate([r[...] for r in v_refs])
    seg = seg_ref[...]
    ks = [jnp.concatenate(x) for x in zip(*[both_masks(r[...], seg) for r in k_refs])]
    for t in range(n // tq):
        rows = pl.ds(t * tq, tq)
        q = q_ref[rows, :] * jnp.asarray(0.125, bf)
        lq = lanes(q.shape) < HD
        segq = seg_ref[rows, :]
        outs, lses = [], []
        for h in range(2):
            feats = mask_feats_q(segq, HD if h == 0 else 0).astype(bf)
            qq = jnp.where(lq, q, feats) if h == 0 else jnp.where(lq, feats, q)
            s = nt(qq, ks[h])
            m = jnp.max(s, axis=-1, keepdims=True)
            p = jnp.exp(s - m)
            l = jnp.sum(p, axis=-1, keepdims=True)
            o = nn(p.astype(bf), v)
            outs.append(o / l)
            lses.append(m + jnp.log(l))
        o_ref[rows, :] = jnp.where(lq, outs[0], outs[1]).astype(bf)
        lse_ref[rows, :] = jnp.where(
            lq, jnp.broadcast_to(lses[0], q.shape), jnp.broadcast_to(lses[1], q.shape)
        )


def specs(n, first, count):
    wide = pl.BlockSpec((n, 2 * HD), lambda h: (0, h + first))
    key = pl.BlockSpec((n, 2 * HD), lambda h: (0, h))
    val = pl.BlockSpec((n, 2 * HD), lambda h: (0, h + count))
    seg = pl.BlockSpec((n, 1), lambda h: (0, 0))
    return wide, key, val, seg


def attn_fwd(q, blocks, seg, first, count, tq=256):
    n = q.shape[0]
    parts, d = len(blocks), count * 2 * HD
    wide, key, val, one = specs(n, first, count)
    return pl.pallas_call(
        functools.partial(fwd_kernel, tq=min(tq, n), parts=parts),
        grid=(count,),
        in_specs=[wide, one] + [key] * parts + [val] * parts,
        out_specs=[key, key],
        out_shape=[jax.ShapeDtypeStruct((n, d), bf), jax.ShapeDtypeStruct((n, d), f32)],
        cost_estimate=pl.CostEstimate(
            flops=16 * n * n * parts * d, bytes_accessed=n * d * (8 + 4 * parts), transcendentals=0
        ),
        name="attn_fwd",
    )(q, seg[:, None], *blocks, *blocks)


def bwd_kernel(*refs, tq, parts):
    q_ref, do_ref, o_ref, lse_ref, seg_ref = refs[:5]
    k_refs, v_refs = refs[5 : 5 + parts], refs[5 + parts : 5 + 2 * parts]
    dq_ref = refs[5 + 2 * parts]
    dkv_refs = refs[6 + 2 * parts : 6 + 3 * parts]
    acc_ref = refs[6 + 3 * parts]
    n = q_ref.shape[0]
    seg = seg_ref[...]
    group = min(2, parts)
    for c in range(0, parts, group):
        k = jnp.concatenate([r[...] for r in k_refs[c : c + group]])
        v = jnp.concatenate([r[...] for r in v_refs[c : c + group]])
        ks = both_masks(k, jnp.concatenate([seg] * group))
        lk = lanes(k.shape) < HD
        z = jnp.zeros_like(k)
        km = [jnp.where(lk, k, z), jnp.where(lk, z, k)]
        dk = jnp.zeros(k.shape, f32)
        dv = jnp.zeros(k.shape, f32)
        for t in range(n // tq):
            rows = pl.ds(t * tq, tq)
            q = q_ref[rows, :] * jnp.asarray(0.125, bf)
            do = do_ref[rows, :]
            lq = lanes(q.shape) < HD
            zq = jnp.zeros_like(q)
            segq = seg_ref[rows, :]
            lse = lse_ref[rows, :]
            prod = do.astype(f32) * o_ref[rows, :].astype(f32)
            dqs = None
            for h in range(2):
                own = lq if h == 0 else ~lq
                qq = jnp.where(own, q, mask_feats_q(segq, HD if h == 0 else 0).astype(bf))
                qm = jnp.where(own, q, zq)
                dom = jnp.where(own, do, zq)
                dd = jnp.sum(jnp.where(own, prod, 0.0), axis=-1, keepdims=True)
                ls = lse[:, :1] if h == 0 else lse[:, HD : HD + 1]
                p = jnp.exp(nt(qq, ks[h]) - ls)
                ds = (p * (nt(dom, v) - dd)).astype(bf)
                dv = dv + tn(p.astype(bf), dom)
                dk = dk + tn(ds, qm)
                x = nn(ds, km[h])
                dqs = x if dqs is None else dqs + x
            if c == 0:
                acc_ref[rows, :] = dqs
            else:
                acc_ref[rows, :] += dqs
        for i in range(group):
            dkv_refs[c + i][0] = dk[i * n : (i + 1) * n].astype(bf)
            dkv_refs[c + i][1] = dv[i * n : (i + 1) * n].astype(bf)
    dq_ref[...] = (acc_ref[...] * 0.125).astype(bf)


def attn_bwd(q, blocks, do, o, lse, seg, first, count, tq=256):
    n = q.shape[0]
    parts, d = len(blocks), count * 2 * HD
    wide, key, val, one = specs(n, first, count)
    pair = pl.BlockSpec((2, n, 2 * HD), lambda h: (0, 0, h))
    return pl.pallas_call(
        functools.partial(bwd_kernel, tq=min(tq, n), parts=parts),
        grid=(count,),
        in_specs=[wide, wide, key, key, one] + [key] * parts + [val] * parts,
        out_specs=[key] + [pair] * parts,
        out_shape=[jax.ShapeDtypeStruct((n, d), bf)] + [jax.ShapeDtypeStruct((2, n, d), bf)] * parts,
        scratch_shapes=[pltpu.VMEM((n, 2 * HD), f32)],
        cost_estimate=pl.CostEstimate(
            flops=40 * n * n * parts * d, bytes_accessed=n * d * (12 + 8 * parts), transcendentals=0
        ),
        name="attn_bwd",
    )(q, do, o, lse, seg[:, None], *blocks, *blocks)


def normed(value, gain, shift):
    center = value - jnp.mean(value, axis=-1, keepdims=True)
    spread = jnp.mean(center * center, axis=-1, keepdims=True)
    return center * lax.rsqrt(spread + 1e-06) * gain + shift


def gelu_tanh(value):
    return jax.nn.gelu(value, approximate=True)


def swap(x, flip):
    parts = lax.axis_size("band")
    return lax.ppermute(x, "band", [(i, i ^ flip) for i in range(parts)])


def spread(blocks, flip):
    while flip >= 1:
        blocks = blocks + [swap(block, flip) for block in blocks]
        flip //= 2
    return blocks


def tie(first, second):
    return lax.optimization_barrier((first, second))


def fold(blocks, flip):
    half = len(blocks) // 2
    return [
        (near.astype(f32) + swap(far, flip).astype(f32)).astype(bf)
        for near, far in zip(blocks[:half], blocks[half:])
    ]


def reduce_relative(blocks, flip=1):
    while len(blocks) > 1:
        blocks = fold(blocks, flip)
        flip *= 2
    return blocks[0]


def gather_vectors(shards):
    packed = jnp.concatenate(shards)
    whole = lax.all_gather(packed, "band", axis=0, tiled=False)
    out, at = [], 0
    for shard in shards:
        out.append(whole[:, at : at + shard.shape[0]].reshape(-1).astype(f32))
        at += shard.shape[0]
    return out


def relative_rows(array):
    me = lax.axis_index("band")
    order = [0]
    flip = lax.axis_size("band") // 2
    while flip >= 1:
        order = order + [i ^ flip for i in order]
        flip //= 2
    return [lax.dynamic_index_in_dim(array, me ^ i, 0, keepdims=False) for i in order]


def reduce_last(matrix, grads, shards):
    parts, columns = lax.axis_size("band"), matrix.shape[1]
    packed = jnp.concatenate([g.reshape(parts, -1) for g in grads], axis=1).astype(bf)
    rows = -(-packed.shape[1] // (16 * columns)) * 16
    packed = jnp.pad(packed, ((0, 0), (0, rows * columns - packed.shape[1])))
    mine = reduce_chip(reduce_core(matrix.astype(bf)))
    extra = reduce_relative(relative_rows(packed.reshape(parts, rows, columns)))
    vector = sum_small(extra).reshape(-1)
    total = finish(mine, 1)
    out, at = [], 0
    for shard in shards:
        out.append(vector[at : at + shard.shape[0]])
        at += shard.shape[0]
    return total, out


def gather_matrix(shard):
    return lax.all_gather(shard, "band", axis=0, tiled=True)


def reduce_core(grad):
    blocks = grad.reshape(lax.axis_size("band"), -1, grad.shape[1])
    return fold(relative_rows(blocks), 1)


def reduce_chip(blocks):
    return reduce_relative(blocks, 2)


def trade(x, flip):
    size = lax.axis_size("dp")
    return lax.ppermute(x, "dp", [(i, i ^ flip) for i in range(size)])


def halve(x, flip):
    bit = lax.rem(lax.axis_index("dp") // flip, 2)
    halves = x.reshape(2, -1, x.shape[1])
    near = lax.dynamic_index_in_dim(halves, bit, 0, keepdims=False)
    far = lax.dynamic_index_in_dim(halves, 1 - bit, 0, keepdims=False)
    return (near.astype(f32) + trade(far, flip).astype(f32)).astype(bf)


def join(x, flip):
    bit = lax.rem(lax.axis_index("dp") // flip, 2)
    other = trade(x, flip)
    return jnp.where(bit == 0, jnp.concatenate([x, other]), jnp.concatenate([other, x]))


def finish(x, flip):
    size = lax.axis_size("dp")
    while flip < size:
        x = halve(x, flip)
        flip *= 2
    while flip > 1:
        flip //= 2
        x = join(x, flip)
    return x.astype(f32)


def sum_small(x):
    flip = 1
    while flip < lax.axis_size("dp"):
        x = (x.astype(f32) + trade(x, flip).astype(f32)).astype(bf)
        flip *= 2
    return x.astype(f32)


def layer(inputs, segments, cotangent, ln1_gain, ln1_bias, w_qkv, b_qv, w_out, b_out, ln2_gain, ln2_bias, w_up, b_up, w_down, b_down):
    micro, tokens, width = inputs.shape[0], inputs.shape[2], inputs.shape[3]
    parts = lax.axis_size("band")
    vectors = (ln1_gain, ln1_bias, b_qv, b_out, ln2_gain, ln2_bias, b_up, b_down)
    gain_one, shift_one, bias_qv, bias_out, gain_two, shift_two, bias_up, bias_down = gather_vectors(vectors)
    w_proj = gather_matrix(w_qkv)

    value = inputs.reshape(micro * tokens, width).astype(f32)
    seg = segments.reshape(micro, tokens)
    normed_in, pull_one = jax.vjp(normed, value, gain_one, shift_one)
    normed_low = normed_in.astype(bf)
    projected = nn(normed_low, w_proj)
    query = (projected[:, :width] + bias_qv[:width]).astype(bf)
    keys = projected[:, width : 2 * width].astype(bf)
    values = (projected[:, 2 * width :] + bias_qv[width:]).astype(bf)

    count = width // (4 * HD)
    half = width // 2
    far = parts // 2
    units = [(m, first) for m in range(micro) for first in (0, count)]
    started = []
    for i, (m, first) in enumerate(units):
        rows, cols = slice(m * tokens, (m + 1) * tokens), slice(first * 2 * HD, first * 2 * HD + half)
        own = jnp.concatenate([keys[rows, cols], values[rows, cols]], axis=1)
        if i > 0:
            started[i - 1], own = tie(started[i - 1], own)
        started.append(own)
    for i, own in enumerate(started):
        started[i] = [own, swap(own, far)]

    saved, mixes = [], []
    for i, (m, first) in enumerate(units):
        blocks = started[i]
        if i > 0:
            blocks, mixes[i - 1] = tie(blocks, mixes[i - 1])
        blocks = spread(blocks, far // 2)
        if i == 0:
            blocks, (w_out, w_up, w_down) = tie(blocks, (w_out, w_up, w_down))
            w_mix = gather_matrix(w_out)
            w_rise = gather_matrix(w_up)
            w_fall = gather_matrix(w_down)
        q = query[m * tokens : (m + 1) * tokens]
        mix, log_total = attn_fwd(q, blocks, seg[m], first, count)
        mixes.append(mix)
        saved.append((q, blocks, mix, log_total, seg[m]))
    mixed = jnp.concatenate(
        [jnp.concatenate(mixes[i : i + 2], axis=1) for i in range(0, 2 * micro, 2)]
    )

    hidden = value + (nn(mixed, w_mix) + bias_out)
    normed_mid, pull_two = jax.vjp(normed, hidden, gain_two, shift_two)
    mid_low = normed_mid.astype(bf)
    upward = nn(mid_low, w_rise) + bias_up
    active, pull_gelu = jax.vjp(gelu_tanh, upward)
    active_low = active.astype(bf)

    real = (seg.reshape(-1, 1) != 0).astype(f32)
    grad_y = cotangent.reshape(micro * tokens, width).astype(f32) * real
    grad_m = grad_y.astype(bf)
    grad_w_fall = tn(active_low, grad_m)
    grad_b_fall = jnp.sum(grad_m.astype(f32), axis=0)
    low_fall, grad_m = tie(grad_w_fall.astype(bf), grad_m)
    fall = reduce_core(low_fall)
    grad_up = pull_gelu(nt(grad_m, w_fall))[0].astype(bf)
    fall, grad_up = tie(fall, grad_up)
    fall = reduce_chip(fall)
    grad_w_rise = tn(mid_low, grad_up)
    grad_mid, grad_gain_two, grad_shift_two = pull_two(nt(grad_up, w_rise))
    grad_hidden = grad_y + grad_mid
    grad_a = grad_hidden.astype(bf)
    grad_w_mix = tn(mixed, grad_a)
    grad_b_mix = jnp.sum(grad_a.astype(f32), axis=0)
    grad_mixed = nt(grad_a, w_mix).astype(bf)

    grad_mixed, *rest = lax.optimization_barrier((grad_mixed, grad_w_rise.astype(bf), grad_w_mix.astype(bf)))
    rise, out_grad = reduce_core(rest[0]), reduce_core(rest[1])

    halves, grads_q = [], []
    for i, (m, first) in enumerate(units):
        q, blocks, mix, log_total, seg_q = saved[i]
        grad_out = grad_mixed[m * tokens : (m + 1) * tokens]
        if i >= 2:
            halves[i - 2], grad_out = tie(halves[i - 2], grad_out)
        if i == 1:
            (fall, rise, out_grad), grad_out = tie((fall, rise, out_grad), grad_out)
            rise, out_grad = reduce_chip(rise), reduce_chip(out_grad)
        if i == 3:
            (fall, rise, out_grad), grad_out = tie((fall, rise, out_grad), grad_out)
            wide = [lax.psum(part, "dp") for part in (fall, rise, out_grad)]
        grad_q, *grad_blocks = attn_bwd(q, blocks, grad_out, mix, log_total, seg_q, first, count)
        halves.append(fold(grad_blocks, 1))
        grads_q.append(grad_q)
    halves[-1], (active_low, grad_up) = tie(halves[-1], (active_low, grad_up))
    output = (hidden + (nn(active_low, w_fall) + bias_down)).astype(bf)
    grad_b_rise = jnp.sum(grad_up.astype(f32), axis=0)
    pairs = []
    for half in halves:
        pairs.append(reduce_relative(half, 2))
    pairs, grads_q = tie(pairs, grads_q)
    grad_qkv = jnp.concatenate(
        [
            jnp.concatenate(
                [grads_q[i], grads_q[i + 1], pairs[i][0], pairs[i + 1][0], pairs[i][1], pairs[i + 1][1]], axis=1
            )
            for i in range(0, 2 * micro, 2)
        ]
    )
    grad_qkv = lax.optimization_barrier(grad_qkv)
    wide = [part.astype(f32) for part in wide]
    grad_w_proj = tn(normed_low, grad_qkv)
    sums = jnp.sum(grad_qkv.astype(f32), axis=0)
    grad_b_proj = jnp.concatenate([sums[:width], sums[2 * width :]])
    grad_norm_in, grad_gain_one, grad_shift_one = pull_one(nt(grad_qkv, w_proj))
    input_grad = (grad_hidden + grad_norm_in).astype(bf)

    last, small = reduce_last(
        grad_w_proj,
        (grad_gain_one, grad_shift_one, grad_b_proj, grad_b_mix, grad_gain_two, grad_shift_two, grad_b_rise, grad_b_fall),
        vectors,
    )
    return (
        output.reshape(inputs.shape),
        input_grad.reshape(inputs.shape),
        small[0],
        small[1],
        last,
        small[2],
        wide[2],
        small[3],
        small[4],
        small[5],
        wide[1],
        small[6],
        wide[0],
        small[7],
    )


def solution(mesh):
    split = P(None, "dp", "band", None)
    rows, vector = P("band", None), P("band")
    weights = (vector, vector, rows, vector, rows, vector, vector, vector, rows, vector, rows, vector)
    return jax.shard_map(
        layer,
        mesh=mesh,
        in_specs=(split, P(None, "dp", "band"), split) + weights,
        out_specs=(split, split) + weights,
        check_vma=False,
    )
```

```python
import functools

import jax
import jax.numpy as jnp
from jax import lax
from jax.sharding import PartitionSpec as P
from jax.experimental import pallas as pl
from jax.experimental.pallas import tpu as pltpu
bf=jnp.bfloat16; f32=jnp.float32
HD=64


def nt(a,b): return lax.dot_general(a,b,(((1,),(1,)),((),())),preferred_element_type=f32)


def nn(a,b): return lax.dot_general(a,b,(((1,),(0,)),((),())),preferred_element_type=f32)


def tn(a,b): return lax.dot_general(a,b,(((0,),(0,)),((),())),preferred_element_type=f32)


def lanes(shape): return lax.broadcasted_iota(jnp.int32,shape,1)


NEG=-1e30


def mask_feats_q(seg, base):
    l=lanes((seg.shape[0],2*HD))
    return (l==seg+base).astype(f32)


def mask_feats_k(seg, base):
    l=lanes((seg.shape[0],2*HD))
    inr=(l>=base)&(l<base+8)
    return jnp.where(inr&(l!=seg+base),NEG,0.0)


def both_masks(k, segk):
    low = lanes(k.shape) < HD
    return [
        jnp.where(low, k, mask_feats_k(segk, HD).astype(bf)),
        jnp.where(low, mask_feats_k(segk, 0).astype(bf), k),
    ]


def fwd_kernel(*refs, tq, parts):
    q_ref, seg_ref = refs[0], refs[1]
    k_refs, v_refs = refs[2 : 2 + parts], refs[2 + parts : 2 + 2 * parts]
    o_ref, lse_ref = refs[2 + 2 * parts :]
    n = q_ref.shape[0]
    v = jnp.concatenate([r[...] for r in v_refs])
    seg = seg_ref[...]
    ks = [jnp.concatenate(x) for x in zip(*[both_masks(r[...], seg) for r in k_refs])]
    for t in range(n // tq):
        rows = pl.ds(t * tq, tq)
        q = q_ref[rows, :] * jnp.asarray(0.125, bf)
        lq = lanes(q.shape) < HD
        segq = seg_ref[rows, :]
        outs, lses = [], []
        for h in range(2):
            feats = mask_feats_q(segq, HD if h == 0 else 0).astype(bf)
            qq = jnp.where(lq, q, feats) if h == 0 else jnp.where(lq, feats, q)
            s = nt(qq, ks[h])
            m = jnp.max(s, axis=-1, keepdims=True)
            p = jnp.exp(s - m)
            l = jnp.sum(p, axis=-1, keepdims=True)
            o = nn(p.astype(bf), v)
            outs.append(o / l)
            lses.append(m + jnp.log(l))
        o_ref[rows, :] = jnp.where(lq, outs[0], outs[1]).astype(bf)
        lse_ref[rows, :] = jnp.where(
            lq, jnp.broadcast_to(lses[0], q.shape), jnp.broadcast_to(lses[1], q.shape)
        )


def specs(n, first, count):
    wide = pl.BlockSpec((n, 2 * HD), lambda h: (0, h + first))
    key = pl.BlockSpec((n, 2 * HD), lambda h: (0, h))
    val = pl.BlockSpec((n, 2 * HD), lambda h: (0, h + count))
    seg = pl.BlockSpec((n, 1), lambda h: (0, 0))
    return wide, key, val, seg


def attn_fwd(q, blocks, seg, first, count, tq=256):
    n = q.shape[0]
    parts, d = len(blocks), count * 2 * HD
    wide, key, val, one = specs(n, first, count)
    return pl.pallas_call(
        functools.partial(fwd_kernel, tq=min(tq, n), parts=parts),
        grid=(count,),
        in_specs=[wide, one] + [key] * parts + [val] * parts,
        out_specs=[key, key],
        out_shape=[jax.ShapeDtypeStruct((n, d), bf), jax.ShapeDtypeStruct((n, d), f32)],
        cost_estimate=pl.CostEstimate(
            flops=16 * n * n * parts * d, bytes_accessed=n * d * (8 + 4 * parts), transcendentals=0
        ),
        name="attn_fwd",
    )(q, seg[:, None], *blocks, *blocks)


def bwd_kernel(*refs, tq, parts):
    q_ref, do_ref, o_ref, lse_ref, seg_ref = refs[:5]
    k_refs, v_refs = refs[5 : 5 + parts], refs[5 + parts : 5 + 2 * parts]
    dq_ref = refs[5 + 2 * parts]
    dkv_refs = refs[6 + 2 * parts : 6 + 3 * parts]
    acc_ref = refs[6 + 3 * parts]
    n = q_ref.shape[0]
    seg = seg_ref[...]
    group = min(2, parts)
    for c in range(0, parts, group):
        k = jnp.concatenate([r[...] for r in k_refs[c : c + group]])
        v = jnp.concatenate([r[...] for r in v_refs[c : c + group]])
        ks = both_masks(k, jnp.concatenate([seg] * group))
        lk = lanes(k.shape) < HD
        z = jnp.zeros_like(k)
        km = [jnp.where(lk, k, z), jnp.where(lk, z, k)]
        dk = jnp.zeros(k.shape, f32)
        dv = jnp.zeros(k.shape, f32)
        for t in range(n // tq):
            rows = pl.ds(t * tq, tq)
            q = q_ref[rows, :] * jnp.asarray(0.125, bf)
            do = do_ref[rows, :]
            lq = lanes(q.shape) < HD
            zq = jnp.zeros_like(q)
            segq = seg_ref[rows, :]
            lse = lse_ref[rows, :]
            prod = do.astype(f32) * o_ref[rows, :].astype(f32)
            dqs = None
            for h in range(2):
                own = lq if h == 0 else ~lq
                qq = jnp.where(own, q, mask_feats_q(segq, HD if h == 0 else 0).astype(bf))
                qm = jnp.where(own, q, zq)
                dom = jnp.where(own, do, zq)
                dd = jnp.sum(jnp.where(own, prod, 0.0), axis=-1, keepdims=True)
                ls = lse[:, :1] if h == 0 else lse[:, HD : HD + 1]
                p = jnp.exp(nt(qq, ks[h]) - ls)
                ds = (p * (nt(dom, v) - dd)).astype(bf)
                dv = dv + tn(p.astype(bf), dom)
                dk = dk + tn(ds, qm)
                x = nn(ds, km[h])
                dqs = x if dqs is None else dqs + x
            if c == 0:
                acc_ref[rows, :] = dqs
            else:
                acc_ref[rows, :] += dqs
        for i in range(group):
            dkv_refs[c + i][0] = dk[i * n : (i + 1) * n].astype(bf)
            dkv_refs[c + i][1] = dv[i * n : (i + 1) * n].astype(bf)
    dq_ref[...] = (acc_ref[...] * 0.125).astype(bf)


def attn_bwd(q, blocks, do, o, lse, seg, first, count, tq=256):
    n = q.shape[0]
    parts, d = len(blocks), count * 2 * HD
    wide, key, val, one = specs(n, first, count)
    pair = pl.BlockSpec((2, n, 2 * HD), lambda h: (0, 0, h))
    return pl.pallas_call(
        functools.partial(bwd_kernel, tq=min(tq, n), parts=parts),
        grid=(count,),
        in_specs=[wide, wide, key, key, one] + [key] * parts + [val] * parts,
        out_specs=[key] + [pair] * parts,
        out_shape=[jax.ShapeDtypeStruct((n, d), bf)] + [jax.ShapeDtypeStruct((2, n, d), bf)] * parts,
        scratch_shapes=[pltpu.VMEM((n, 2 * HD), f32)],
        cost_estimate=pl.CostEstimate(
            flops=40 * n * n * parts * d, bytes_accessed=n * d * (12 + 8 * parts), transcendentals=0
        ),
        name="attn_bwd",
    )(q, do, o, lse, seg[:, None], *blocks, *blocks)


def normed(value, gain, shift):
    center = value - jnp.mean(value, axis=-1, keepdims=True)
    spread = jnp.mean(center * center, axis=-1, keepdims=True)
    return center * lax.rsqrt(spread + 1e-06) * gain + shift


def gelu_tanh(value):
    return jax.nn.gelu(value, approximate=True)


def swap(x, flip):
    parts = lax.axis_size("band")
    return lax.ppermute(x, "band", [(i, i ^ flip) for i in range(parts)])


def spread(blocks, flip):
    while flip >= 1:
        blocks = blocks + [swap(block, flip) for block in blocks]
        flip //= 2
    return blocks


def tie(first, second):
    return lax.optimization_barrier((first, second))


def fold(blocks, flip):
    half = len(blocks) // 2
    return [
        (near.astype(f32) + swap(far, flip).astype(f32)).astype(bf)
        for near, far in zip(blocks[:half], blocks[half:])
    ]


def reduce_relative(blocks, flip=1):
    while len(blocks) > 1:
        blocks = fold(blocks, flip)
        flip *= 2
    return blocks[0]


def gather_vectors(shards):
    packed = jnp.concatenate(shards)
    whole = lax.all_gather(packed, "band", axis=0, tiled=False)
    out, at = [], 0
    for shard in shards:
        out.append(whole[:, at : at + shard.shape[0]].reshape(-1).astype(f32))
        at += shard.shape[0]
    return out


def relative_rows(array):
    me = lax.axis_index("band")
    order = [0]
    flip = lax.axis_size("band") // 2
    while flip >= 1:
        order = order + [i ^ flip for i in order]
        flip //= 2
    return [lax.dynamic_index_in_dim(array, me ^ i, 0, keepdims=False) for i in order]


def reduce_last(matrix, grads, shards):
    parts, columns = lax.axis_size("band"), matrix.shape[1]
    packed = jnp.concatenate([g.reshape(parts, -1) for g in grads], axis=1).astype(bf)
    rows = -(-packed.shape[1] // (16 * columns)) * 16
    packed = jnp.pad(packed, ((0, 0), (0, rows * columns - packed.shape[1])))
    mine = reduce_chip(reduce_core(matrix))
    extra = reduce_relative(relative_rows(packed.reshape(parts, rows, columns)))
    vector = sum_small(extra).reshape(-1)
    total = finish(mine, 1)
    out, at = [], 0
    for shard in shards:
        out.append(vector[at : at + shard.shape[0]])
        at += shard.shape[0]
    return total, out


def gather_matrix(shard):
    return lax.all_gather(shard, "band", axis=0, tiled=True)


def reduce_core(grad):
    blocks = grad.reshape(lax.axis_size("band"), -1, grad.shape[1])
    return fold(relative_rows(blocks), 1)


def reduce_chip(blocks):
    return reduce_relative(blocks, 2)


def trade(x, flip):
    size = lax.axis_size("dp")
    return lax.ppermute(x, "dp", [(i, i ^ flip) for i in range(size)])


def halve(x, flip):
    bit = lax.rem(lax.axis_index("dp") // flip, 2)
    halves = x.reshape(2, -1, x.shape[1])
    near = lax.dynamic_index_in_dim(halves, bit, 0, keepdims=False)
    far = lax.dynamic_index_in_dim(halves, 1 - bit, 0, keepdims=False)
    return (near.astype(f32) + trade(far, flip).astype(f32)).astype(bf)


def join(x, flip):
    bit = lax.rem(lax.axis_index("dp") // flip, 2)
    other = trade(x, flip)
    return jnp.where(bit == 0, jnp.concatenate([x, other]), jnp.concatenate([other, x]))


def finish(x, flip):
    size = lax.axis_size("dp")
    while flip < size:
        x = halve(x, flip)
        flip *= 2
    while flip > 1:
        flip //= 2
        x = join(x, flip)
    return x.astype(f32)


def sum_small(x):
    flip = 1
    while flip < lax.axis_size("dp"):
        x = (x.astype(f32) + trade(x, flip).astype(f32)).astype(bf)
        flip *= 2
    return x.astype(f32)


def layer(inputs, segments, cotangent, ln1_gain, ln1_bias, w_qkv, b_qv, w_out, b_out, ln2_gain, ln2_bias, w_up, b_up, w_down, b_down):
    micro, tokens, width = inputs.shape[0], inputs.shape[2], inputs.shape[3]
    parts = lax.axis_size("band")
    vectors = (ln1_gain, ln1_bias, b_qv, b_out, ln2_gain, ln2_bias, b_up, b_down)
    gain_one, shift_one, bias_qv, bias_out, gain_two, shift_two, bias_up, bias_down = gather_vectors(vectors)
    w_proj = gather_matrix(w_qkv)

    value = inputs.reshape(micro * tokens, width).astype(f32)
    seg = segments.reshape(micro, tokens)
    normed_in, pull_one = jax.vjp(normed, value, gain_one, shift_one)
    normed_low = normed_in.astype(bf)
    projected = nn(normed_low, w_proj)
    query = (projected[:, :width] + bias_qv[:width]).astype(bf)
    keys = projected[:, width : 2 * width].astype(bf)
    values = (projected[:, 2 * width :] + bias_qv[width:]).astype(bf)

    count = width // (4 * HD)
    half = width // 2
    far = parts // 2
    units = [(m, first) for m in range(micro) for first in (0, count)]
    started = []
    for i, (m, first) in enumerate(units):
        rows, cols = slice(m * tokens, (m + 1) * tokens), slice(first * 2 * HD, first * 2 * HD + half)
        own = jnp.concatenate([keys[rows, cols], values[rows, cols]], axis=1)
        if i > 0:
            started[i - 1], own = tie(started[i - 1], own)
        started.append(own)
    for i, own in enumerate(started):
        started[i] = [own, swap(own, far)]

    saved, mixes = [], []
    for i, (m, first) in enumerate(units):
        blocks = started[i]
        if i > 0:
            blocks, mixes[i - 1] = tie(blocks, mixes[i - 1])
        blocks = spread(blocks, far // 2)
        if i == 0:
            blocks, (w_out, w_up, w_down) = tie(blocks, (w_out, w_up, w_down))
            w_mix = gather_matrix(w_out)
            w_rise = gather_matrix(w_up)
            w_fall = gather_matrix(w_down)
        q = query[m * tokens : (m + 1) * tokens]
        mix, log_total = attn_fwd(q, blocks, seg[m], first, count)
        mixes.append(mix)
        saved.append((q, blocks, mix, log_total, seg[m]))
    mixed = jnp.concatenate(
        [jnp.concatenate(mixes[i : i + 2], axis=1) for i in range(0, 2 * micro, 2)]
    )

    hidden = value + (nn(mixed, w_mix) + bias_out)
    normed_mid, pull_two = jax.vjp(normed, hidden, gain_two, shift_two)
    mid_low = normed_mid.astype(bf)
    upward = nn(mid_low, w_rise) + bias_up
    active, pull_gelu = jax.vjp(gelu_tanh, upward)
    active_low = active.astype(bf)

    real = (seg.reshape(-1, 1) != 0).astype(f32)
    grad_y = cotangent.reshape(micro * tokens, width).astype(f32) * real
    grad_m = grad_y.astype(bf)
    grad_w_fall = tn(active_low, grad_m)
    grad_b_fall = jnp.sum(grad_m.astype(f32), axis=0)
    low_fall, grad_m = tie(grad_w_fall.astype(bf), grad_m)
    fall = reduce_core(low_fall)
    grad_up = pull_gelu(nt(grad_m, w_fall))[0].astype(bf)
    fall, grad_up = tie(fall, grad_up)
    fall = reduce_chip(fall)
    grad_w_rise = tn(mid_low, grad_up)
    low_rise, grad_up = tie(grad_w_rise.astype(bf), grad_up)
    rise = reduce_core(low_rise)
    grad_mid, grad_gain_two, grad_shift_two = pull_two(nt(grad_up, w_rise))
    grad_hidden = grad_y + grad_mid
    grad_a = grad_hidden.astype(bf)
    grad_w_mix = tn(mixed, grad_a)
    grad_b_mix = jnp.sum(grad_a.astype(f32), axis=0)
    grad_mixed = nt(grad_a, w_mix).astype(bf)

    (rise, low_out), grad_mixed = tie((rise, grad_w_mix.astype(bf)), grad_mixed)
    rise, out_grad = reduce_chip(rise), reduce_core(low_out)

    halves, grads_q = [], []
    for i, (m, first) in enumerate(units):
        q, blocks, mix, log_total, seg_q = saved[i]
        grad_out = grad_mixed[m * tokens : (m + 1) * tokens]
        if i >= 2:
            halves[i - 2], grad_out = tie(halves[i - 2], grad_out)
        if i == 1:
            (fall, out_grad), grad_out = tie((fall, out_grad), grad_out)
            out_grad = reduce_chip(out_grad)
        if i == 3:
            (fall, rise, out_grad), grad_out = tie((fall, rise, out_grad), grad_out)
            wide = [lax.psum(part, "dp") for part in (fall, rise, out_grad)]
        grad_q, *grad_blocks = attn_bwd(q, blocks, grad_out, mix, log_total, seg_q, first, count)
        halves.append(fold(grad_blocks, 1))
        grads_q.append(grad_q)
    halves[-1], (active_low, grad_up) = tie(halves[-1], (active_low, grad_up))
    output = (hidden + (nn(active_low, w_fall) + bias_down)).astype(bf)
    grad_b_rise = jnp.sum(grad_up.astype(f32), axis=0)
    pairs = []
    for half in halves:
        pairs.append(reduce_relative(half, 2))
    pairs, grads_q = tie(pairs, grads_q)
    grad_qkv = jnp.concatenate(
        [
            jnp.concatenate(
                [grads_q[i], grads_q[i + 1], pairs[i][0], pairs[i + 1][0], pairs[i][1], pairs[i + 1][1]], axis=1
            )
            for i in range(0, 2 * micro, 2)
        ]
    )
    grad_qkv = lax.optimization_barrier(grad_qkv)
    wide = [part.astype(f32) for part in wide]
    grad_w_proj = tn(normed_low, grad_qkv)
    low_proj, grad_qkv = tie(grad_w_proj.astype(bf), grad_qkv)
    sums = jnp.sum(grad_qkv.astype(f32), axis=0)
    grad_b_proj = jnp.concatenate([sums[:width], sums[2 * width :]])
    grad_norm_in, grad_gain_one, grad_shift_one = pull_one(nt(grad_qkv, w_proj))
    input_grad = (grad_hidden + grad_norm_in).astype(bf)

    last, small = reduce_last(
        low_proj,
        (grad_gain_one, grad_shift_one, grad_b_proj, grad_b_mix, grad_gain_two, grad_shift_two, grad_b_rise, grad_b_fall),
        vectors,
    )
    return (
        output.reshape(inputs.shape),
        input_grad.reshape(inputs.shape),
        small[0],
        small[1],
        last,
        small[2],
        wide[2],
        small[3],
        small[4],
        small[5],
        wide[1],
        small[6],
        wide[0],
        small[7],
    )


def solution(mesh):
    split = P(None, "dp", "band", None)
    rows, vector = P("band", None), P("band")
    weights = (vector, vector, rows, vector, rows, vector, vector, vector, rows, vector, rows, vector)
    return jax.shard_map(
        layer,
        mesh=mesh,
        in_specs=(split, P(None, "dp", "band"), split) + weights,
        out_specs=(split, split) + weights,
        check_vma=False,
    )
```

```python
import functools
import math

import jax
import jax.numpy as jnp
from jax import lax
from jax.sharding import PartitionSpec as P
from jax.experimental import pallas as pl
from jax.experimental.pallas import tpu as pltpu
bf=jnp.bfloat16; f32=jnp.float32
HD=64


def nt(a,b): return lax.dot_general(a,b,(((1,),(1,)),((),())),preferred_element_type=f32)


def nn(a,b): return lax.dot_general(a,b,(((1,),(0,)),((),())),preferred_element_type=f32)


def tn(a,b): return lax.dot_general(a,b,(((0,),(0,)),((),())),preferred_element_type=f32)


def lanes(shape): return lax.broadcasted_iota(jnp.int32,shape,1)


NEG=-1e30


def mask_feats_q(seg, base):
    l=lanes((seg.shape[0],2*HD))
    return (l==seg+base).astype(f32)


def mask_feats_k(seg, base):
    l=lanes((seg.shape[0],2*HD))
    inr=(l>=base)&(l<base+8)
    return jnp.where(inr&(l!=seg+base),NEG,0.0)


def both_masks(k, segk):
    low = lanes(k.shape) < HD
    return [
        jnp.where(low, k, mask_feats_k(segk, HD).astype(bf)),
        jnp.where(low, mask_feats_k(segk, 0).astype(bf), k),
    ]


def fwd_kernel(*refs, tq, parts):
    q_ref, seg_ref = refs[0], refs[1]
    k_refs, v_refs = refs[2 : 2 + parts], refs[2 + parts : 2 + 2 * parts]
    o_ref, lse_ref = refs[2 + 2 * parts :]
    n = q_ref.shape[0]
    v = jnp.concatenate([r[...] for r in v_refs])
    seg = seg_ref[...]
    ks = [jnp.concatenate(x) for x in zip(*[both_masks(r[...], seg) for r in k_refs])]
    for t in range(n // tq):
        rows = pl.ds(t * tq, tq)
        q = q_ref[rows, :] * jnp.asarray(0.125, bf)
        lq = lanes(q.shape) < HD
        segq = seg_ref[rows, :]
        outs, lses = [], []
        for h in range(2):
            feats = mask_feats_q(segq, HD if h == 0 else 0).astype(bf)
            qq = jnp.where(lq, q, feats) if h == 0 else jnp.where(lq, feats, q)
            s = nt(qq, ks[h])
            m = jnp.max(s, axis=-1, keepdims=True)
            p = jnp.exp(s - m)
            l = jnp.sum(p, axis=-1, keepdims=True)
            o = nn(p.astype(bf), v)
            outs.append(o / l)
            lses.append(m + jnp.log(l))
        o_ref[rows, :] = jnp.where(lq, outs[0], outs[1]).astype(bf)
        lse_ref[rows, :] = jnp.where(
            lq, jnp.broadcast_to(lses[0], q.shape), jnp.broadcast_to(lses[1], q.shape)
        )


def specs(n, first, count):
    wide = pl.BlockSpec((n, 2 * HD), lambda h: (0, h + first))
    key = pl.BlockSpec((n, 2 * HD), lambda h: (0, h))
    val = pl.BlockSpec((n, 2 * HD), lambda h: (0, h + count))
    seg = pl.BlockSpec((n, 1), lambda h: (0, 0))
    return wide, key, val, seg


def attn_fwd(q, blocks, seg, first, count, tq=256):
    n = q.shape[0]
    parts, d = len(blocks), count * 2 * HD
    wide, key, val, one = specs(n, first, count)
    return pl.pallas_call(
        functools.partial(fwd_kernel, tq=min(tq, n), parts=parts),
        grid=(count,),
        in_specs=[wide, one] + [key] * parts + [val] * parts,
        out_specs=[key, key],
        out_shape=[jax.ShapeDtypeStruct((n, d), bf), jax.ShapeDtypeStruct((n, d), f32)],
        cost_estimate=pl.CostEstimate(
            flops=16 * n * n * parts * d, bytes_accessed=n * d * (8 + 4 * parts), transcendentals=0
        ),
        name="attn_fwd",
    )(q, seg[:, None], *blocks, *blocks)


def bwd_kernel(*refs, tq, parts):
    q_ref, do_ref, o_ref, lse_ref, seg_ref = refs[:5]
    k_refs, v_refs = refs[5 : 5 + parts], refs[5 + parts : 5 + 2 * parts]
    dq_ref = refs[5 + 2 * parts]
    dkv_refs = refs[6 + 2 * parts : 6 + 3 * parts]
    acc_ref = refs[6 + 3 * parts]
    n = q_ref.shape[0]
    seg = seg_ref[...]
    group = min(2, parts)
    for c in range(0, parts, group):
        k = jnp.concatenate([r[...] for r in k_refs[c : c + group]])
        v = jnp.concatenate([r[...] for r in v_refs[c : c + group]])
        ks = both_masks(k, jnp.concatenate([seg] * group))
        lk = lanes(k.shape) < HD
        z = jnp.zeros_like(k)
        km = [jnp.where(lk, k, z), jnp.where(lk, z, k)]
        dk = jnp.zeros(k.shape, f32)
        dv = jnp.zeros(k.shape, f32)
        for t in range(n // tq):
            rows = pl.ds(t * tq, tq)
            q = q_ref[rows, :] * jnp.asarray(0.125, bf)
            do = do_ref[rows, :]
            lq = lanes(q.shape) < HD
            zq = jnp.zeros_like(q)
            segq = seg_ref[rows, :]
            lse = lse_ref[rows, :]
            prod = do.astype(f32) * o_ref[rows, :].astype(f32)
            dqs = None
            for h in range(2):
                own = lq if h == 0 else ~lq
                qq = jnp.where(own, q, mask_feats_q(segq, HD if h == 0 else 0).astype(bf))
                qm = jnp.where(own, q, zq)
                dom = jnp.where(own, do, zq)
                dd = jnp.sum(jnp.where(own, prod, 0.0), axis=-1, keepdims=True)
                ls = lse[:, :1] if h == 0 else lse[:, HD : HD + 1]
                p = jnp.exp(nt(qq, ks[h]) - ls)
                ds = (p * (nt(dom, v) - dd)).astype(bf)
                dv = dv + tn(p.astype(bf), dom)
                dk = dk + tn(ds, qm)
                x = nn(ds, km[h])
                dqs = x if dqs is None else dqs + x
            if c == 0:
                acc_ref[rows, :] = dqs
            else:
                acc_ref[rows, :] += dqs
        for i in range(group):
            dkv_refs[c + i][0] = dk[i * n : (i + 1) * n].astype(bf)
            dkv_refs[c + i][1] = dv[i * n : (i + 1) * n].astype(bf)
    dq_ref[...] = (acc_ref[...] * 0.125).astype(bf)


def attn_bwd(q, blocks, do, o, lse, seg, first, count, tq=256):
    n = q.shape[0]
    parts, d = len(blocks), count * 2 * HD
    wide, key, val, one = specs(n, first, count)
    pair = pl.BlockSpec((2, n, 2 * HD), lambda h: (0, 0, h))
    return pl.pallas_call(
        functools.partial(bwd_kernel, tq=min(tq, n), parts=parts),
        grid=(count,),
        in_specs=[wide, wide, key, key, one] + [key] * parts + [val] * parts,
        out_specs=[key] + [pair] * parts,
        out_shape=[jax.ShapeDtypeStruct((n, d), bf)] + [jax.ShapeDtypeStruct((2, n, d), bf)] * parts,
        scratch_shapes=[pltpu.VMEM((n, 2 * HD), f32)],
        cost_estimate=pl.CostEstimate(
            flops=40 * n * n * parts * d, bytes_accessed=n * d * (12 + 8 * parts), transcendentals=0
        ),
        name="attn_bwd",
    )(q, do, o, lse, seg[:, None], *blocks, *blocks)


def normed(value, gain, shift):
    center = value - jnp.mean(value, axis=-1, keepdims=True)
    spread = jnp.mean(center * center, axis=-1, keepdims=True)
    return center * lax.rsqrt(spread + 1e-06) * gain + shift


GELU = (2 / math.pi) ** 0.5


def swap(x, flip):
    parts = lax.axis_size("band")
    return lax.ppermute(x, "band", [(i, i ^ flip) for i in range(parts)])


def spread(blocks, flip):
    while flip >= 1:
        blocks = blocks + [swap(block, flip) for block in blocks]
        flip //= 2
    return blocks


def tie(first, second):
    return lax.optimization_barrier((first, second))


def fold(blocks, flip):
    half = len(blocks) // 2
    return [
        (near.astype(f32) + swap(far, flip).astype(f32)).astype(bf)
        for near, far in zip(blocks[:half], blocks[half:])
    ]


def reduce_relative(blocks, flip=1):
    while len(blocks) > 1:
        blocks = fold(blocks, flip)
        flip *= 2
    return blocks[0]


def gather_vectors(shards):
    packed = jnp.concatenate(shards)
    whole = lax.all_gather(packed, "band", axis=0, tiled=False)
    out, at = [], 0
    for shard in shards:
        out.append(whole[:, at : at + shard.shape[0]].reshape(-1).astype(f32))
        at += shard.shape[0]
    return out


def relative_rows(array):
    me = lax.axis_index("band")
    order = [0]
    flip = lax.axis_size("band") // 2
    while flip >= 1:
        order = order + [i ^ flip for i in order]
        flip //= 2
    return [lax.dynamic_index_in_dim(array, me ^ i, 0, keepdims=False) for i in order]


def reduce_last(matrix, grads, shards):
    parts, columns = lax.axis_size("band"), matrix.shape[1]
    packed = jnp.concatenate([g.reshape(parts, -1) for g in grads], axis=1).astype(bf)
    rows = -(-packed.shape[1] // (16 * columns)) * 16
    packed = jnp.pad(packed, ((0, 0), (0, rows * columns - packed.shape[1])))
    mine = reduce_chip(reduce_core(matrix))
    extra = reduce_relative(relative_rows(packed.reshape(parts, rows, columns)))
    vector = sum_small(extra).reshape(-1)
    total = finish(mine, 1)
    out, at = [], 0
    for shard in shards:
        out.append(vector[at : at + shard.shape[0]])
        at += shard.shape[0]
    return total, out


def gather_matrix(shard):
    return lax.all_gather(shard, "band", axis=0, tiled=True)


def reduce_core(grad):
    blocks = grad.reshape(lax.axis_size("band"), -1, grad.shape[1])
    return fold(relative_rows(blocks), 1)


def reduce_chip(blocks):
    return reduce_relative(blocks, 2)


def trade(x, flip):
    size = lax.axis_size("dp")
    return lax.ppermute(x, "dp", [(i, i ^ flip) for i in range(size)])


def halve(x, flip):
    bit = lax.rem(lax.axis_index("dp") // flip, 2)
    halves = x.reshape(2, -1, x.shape[1])
    near = lax.dynamic_index_in_dim(halves, bit, 0, keepdims=False)
    far = lax.dynamic_index_in_dim(halves, 1 - bit, 0, keepdims=False)
    return (near.astype(f32) + trade(far, flip).astype(f32)).astype(bf)


def join(x, flip):
    bit = lax.rem(lax.axis_index("dp") // flip, 2)
    other = trade(x, flip)
    return jnp.where(bit == 0, jnp.concatenate([x, other]), jnp.concatenate([other, x]))


def finish(x, flip):
    size = lax.axis_size("dp")
    while flip < size:
        x = halve(x, flip)
        flip *= 2
    while flip > 1:
        flip //= 2
        x = join(x, flip)
    return x.astype(f32)


def sum_small(x):
    flip = 1
    while flip < lax.axis_size("dp"):
        x = (x.astype(f32) + trade(x, flip).astype(f32)).astype(bf)
        flip *= 2
    return x.astype(f32)


def layer(inputs, segments, cotangent, ln1_gain, ln1_bias, w_qkv, b_qv, w_out, b_out, ln2_gain, ln2_bias, w_up, b_up, w_down, b_down):
    micro, tokens, width = inputs.shape[0], inputs.shape[2], inputs.shape[3]
    parts = lax.axis_size("band")
    vectors = (ln1_gain, ln1_bias, b_qv, b_out, ln2_gain, ln2_bias, b_up, b_down)
    gain_one, shift_one, bias_qv, bias_out, gain_two, shift_two, bias_up, bias_down = gather_vectors(vectors)
    w_proj = gather_matrix(w_qkv)

    value = inputs.reshape(micro * tokens, width).astype(f32)
    seg = segments.reshape(micro, tokens)
    normed_in, pull_one = jax.vjp(normed, value, gain_one, shift_one)
    normed_low = normed_in.astype(bf)
    projected = nn(normed_low, w_proj)
    query = (projected[:, :width] + bias_qv[:width]).astype(bf)
    keys = projected[:, width : 2 * width].astype(bf)
    values = (projected[:, 2 * width :] + bias_qv[width:]).astype(bf)

    count = width // (4 * HD)
    half = width // 2
    far = parts // 2
    units = [(m, first) for m in range(micro) for first in (0, count)]
    started = []
    for i, (m, first) in enumerate(units):
        rows, cols = slice(m * tokens, (m + 1) * tokens), slice(first * 2 * HD, first * 2 * HD + half)
        own = jnp.concatenate([keys[rows, cols], values[rows, cols]], axis=1)
        if i > 0:
            started[i - 1], own = tie(started[i - 1], own)
        started.append(own)
    for i, own in enumerate(started):
        started[i] = [own, swap(own, far)]

    saved, mixes = [], []
    for i, (m, first) in enumerate(units):
        blocks = started[i]
        if i > 0:
            blocks, mixes[i - 1] = tie(blocks, mixes[i - 1])
        blocks = spread(blocks, far // 2)
        if i == 0:
            blocks, (w_out, w_up, w_down) = tie(blocks, (w_out, w_up, w_down))
            w_mix = gather_matrix(w_out)
            w_rise = gather_matrix(w_up)
            w_fall = gather_matrix(w_down)
        q = query[m * tokens : (m + 1) * tokens]
        mix, log_total = attn_fwd(q, blocks, seg[m], first, count)
        mixes.append(mix)
        saved.append((q, blocks, mix, log_total, seg[m]))
    mixed = jnp.concatenate(
        [jnp.concatenate(mixes[i : i + 2], axis=1) for i in range(0, 2 * micro, 2)]
    )

    hidden = value + (nn(mixed, w_mix) + bias_out)
    normed_mid, pull_two = jax.vjp(normed, hidden, gain_two, shift_two)
    mid_low = normed_mid.astype(bf)
    upward = nn(mid_low, w_rise) + bias_up
    bent = jnp.tanh(GELU * (upward + 0.044715 * upward * upward * upward))
    active_low = (0.5 * upward * (1 + bent)).astype(bf)
    slope = 0.5 * (1 + bent) + 0.5 * upward * (1 - bent * bent) * (GELU * (1 + 3 * 0.044715 * upward * upward))
    active_low, slope = lax.optimization_barrier((active_low, slope))

    real = (seg.reshape(-1, 1) != 0).astype(f32)
    grad_y = cotangent.reshape(micro * tokens, width).astype(f32) * real
    grad_m = grad_y.astype(bf)
    grad_w_fall = tn(active_low, grad_m)
    grad_b_fall = jnp.sum(grad_m.astype(f32), axis=0)
    low_fall, grad_m = tie(grad_w_fall.astype(bf), grad_m)
    fall = reduce_core(low_fall)
    grad_up = (nt(grad_m, w_fall) * slope).astype(bf)
    fall, grad_up = tie(fall, grad_up)
    fall = reduce_chip(fall)
    grad_w_rise = tn(mid_low, grad_up)
    low_rise, grad_up = tie(grad_w_rise.astype(bf), grad_up)
    rise = reduce_core(low_rise)
    grad_mid, grad_gain_two, grad_shift_two = pull_two(nt(grad_up, w_rise))
    grad_hidden = grad_y + grad_mid
    grad_a = grad_hidden.astype(bf)
    grad_w_mix = tn(mixed, grad_a)
    grad_b_mix = jnp.sum(grad_a.astype(f32), axis=0)
    grad_mixed = nt(grad_a, w_mix).astype(bf)

    (rise, low_out), grad_mixed = tie((rise, grad_w_mix.astype(bf)), grad_mixed)
    rise, out_grad = reduce_chip(rise), reduce_core(low_out)

    halves, grads_q = [], []
    for i, (m, first) in enumerate(units):
        q, blocks, mix, log_total, seg_q = saved[i]
        grad_out = grad_mixed[m * tokens : (m + 1) * tokens]
        if i >= 2:
            halves[i - 2], grad_out = tie(halves[i - 2], grad_out)
        if i == 1:
            (fall, out_grad), grad_out = tie((fall, out_grad), grad_out)
            out_grad = reduce_chip(out_grad)
        if i == 3:
            (fall, rise, out_grad), grad_out = tie((fall, rise, out_grad), grad_out)
            wide = [lax.psum(part, "dp") for part in (fall, rise, out_grad)]
        grad_q, *grad_blocks = attn_bwd(q, blocks, grad_out, mix, log_total, seg_q, first, count)
        halves.append(fold(grad_blocks, 1))
        grads_q.append(grad_q)
    halves[-1], (active_low, grad_up) = tie(halves[-1], (active_low, grad_up))
    output = (hidden + (nn(active_low, w_fall) + bias_down)).astype(bf)
    grad_b_rise = jnp.sum(grad_up.astype(f32), axis=0)
    pairs = []
    for half in halves:
        pairs.append(reduce_relative(half, 2))
    grad_query = jnp.concatenate(
        [jnp.concatenate(grads_q[i : i + 2], axis=1) for i in range(0, 2 * micro, 2)]
    )
    low_query = tn(normed_low, grad_query).astype(bf)
    query_part = reduce_chip(reduce_core(low_query))
    query_part = finish(query_part, 1)

    pairs = lax.optimization_barrier(pairs)
    grad_pair = jnp.concatenate(
        [
            jnp.concatenate([pairs[i][0], pairs[i + 1][0], pairs[i][1], pairs[i + 1][1]], axis=1)
            for i in range(0, 2 * micro, 2)
        ]
    )
    grad_pair = lax.optimization_barrier(grad_pair)
    wide = [part.astype(f32) for part in wide]
    low_pair, grad_pair = tie(tn(normed_low, grad_pair).astype(bf), grad_pair)
    grad_b_proj = jnp.concatenate(
        [jnp.sum(grad_query.astype(f32), axis=0), jnp.sum(grad_pair[:, width:].astype(f32), axis=0)]
    )
    grad_norm = nt(grad_query, w_proj[:, :width]) + nt(grad_pair, w_proj[:, width:])
    grad_norm_in, grad_gain_one, grad_shift_one = pull_one(grad_norm)
    input_grad = (grad_hidden + grad_norm_in).astype(bf)

    last, small = reduce_last(
        low_pair,
        (grad_gain_one, grad_shift_one, grad_b_proj, grad_b_mix, grad_gain_two, grad_shift_two, grad_b_rise, grad_b_fall),
        vectors,
    )
    last = jnp.concatenate([query_part, last], axis=1)
    return (
        output.reshape(inputs.shape),
        input_grad.reshape(inputs.shape),
        small[0],
        small[1],
        last,
        small[2],
        wide[2],
        small[3],
        small[4],
        small[5],
        wide[1],
        small[6],
        wide[0],
        small[7],
    )


def solution(mesh):
    split = P(None, "dp", "band", None)
    rows, vector = P("band", None), P("band")
    weights = (vector, vector, rows, vector, rows, vector, vector, vector, rows, vector, rows, vector)
    return jax.shard_map(
        layer,
        mesh=mesh,
        in_specs=(split, P(None, "dp", "band"), split) + weights,
        out_specs=(split, split) + weights,
        check_vma=False,
    )
```

```python
import functools
import math

import jax
import jax.numpy as jnp
from jax import lax
from jax.sharding import PartitionSpec as P
from jax.experimental import pallas as pl
from jax.experimental.pallas import tpu as pltpu
bf=jnp.bfloat16; f32=jnp.float32
HD=64


def nt(a,b): return lax.dot_general(a,b,(((1,),(1,)),((),())),preferred_element_type=f32)


def nn(a,b): return lax.dot_general(a,b,(((1,),(0,)),((),())),preferred_element_type=f32)


def tn(a,b): return lax.dot_general(a,b,(((0,),(0,)),((),())),preferred_element_type=f32)


def lanes(shape): return lax.broadcasted_iota(jnp.int32,shape,1)


NEG=-1e30


def mask_feats_q(seg, base):
    l=lanes((seg.shape[0],2*HD))
    return (l==seg+base).astype(f32)


def mask_feats_k(seg, base):
    l=lanes((seg.shape[0],2*HD))
    inr=(l>=base)&(l<base+8)
    return jnp.where(inr&(l!=seg+base),NEG,0.0)


def both_masks(k, segk):
    low = lanes(k.shape) < HD
    return [
        jnp.where(low, k, mask_feats_k(segk, HD).astype(bf)),
        jnp.where(low, mask_feats_k(segk, 0).astype(bf), k),
    ]


def fwd_kernel(*refs, tq, parts):
    q_ref, seg_ref = refs[0], refs[1]
    k_refs, v_refs = refs[2 : 2 + parts], refs[2 + parts : 2 + 2 * parts]
    o_ref, lse_ref = refs[2 + 2 * parts :]
    n = q_ref.shape[0]
    v = jnp.concatenate([r[...] for r in v_refs])
    seg = seg_ref[...]
    ks = [jnp.concatenate(x) for x in zip(*[both_masks(r[...], seg) for r in k_refs])]
    for t in range(n // tq):
        rows = pl.ds(t * tq, tq)
        q = q_ref[rows, :] * jnp.asarray(0.125, bf)
        lq = lanes(q.shape) < HD
        segq = seg_ref[rows, :]
        outs, lses = [], []
        for h in range(2):
            feats = mask_feats_q(segq, HD if h == 0 else 0).astype(bf)
            qq = jnp.where(lq, q, feats) if h == 0 else jnp.where(lq, feats, q)
            s = nt(qq, ks[h])
            m = jnp.max(s, axis=-1, keepdims=True)
            p = jnp.exp(s - m)
            l = jnp.sum(p, axis=-1, keepdims=True)
            o = nn(p.astype(bf), v)
            outs.append(o / l)
            lses.append(m + jnp.log(l))
        o_ref[rows, :] = jnp.where(lq, outs[0], outs[1]).astype(bf)
        lse_ref[rows, :] = jnp.where(
            lq, jnp.broadcast_to(lses[0], q.shape), jnp.broadcast_to(lses[1], q.shape)
        )


def specs(n, first, count):
    wide = pl.BlockSpec((n, 2 * HD), lambda h: (0, h + first))
    key = pl.BlockSpec((n, 2 * HD), lambda h: (0, h))
    val = pl.BlockSpec((n, 2 * HD), lambda h: (0, h + count))
    seg = pl.BlockSpec((n, 1), lambda h: (0, 0))
    return wide, key, val, seg


def attn_fwd(q, blocks, seg, first, count, tq=256):
    n = q.shape[0]
    parts, d = len(blocks), count * 2 * HD
    wide, key, val, one = specs(n, first, count)
    return pl.pallas_call(
        functools.partial(fwd_kernel, tq=min(tq, n), parts=parts),
        grid=(count,),
        in_specs=[wide, one] + [key] * parts + [val] * parts,
        out_specs=[key, key],
        out_shape=[jax.ShapeDtypeStruct((n, d), bf), jax.ShapeDtypeStruct((n, d), f32)],
        cost_estimate=pl.CostEstimate(
            flops=16 * n * n * parts * d, bytes_accessed=n * d * (8 + 4 * parts), transcendentals=0
        ),
        name="attn_fwd",
    )(q, seg[:, None], *blocks, *blocks)


def bwd_kernel(*refs, tq, parts):
    q_ref, do_ref, o_ref, lse_ref, seg_ref = refs[:5]
    k_refs, v_refs = refs[5 : 5 + parts], refs[5 + parts : 5 + 2 * parts]
    dq_ref = refs[5 + 2 * parts]
    dkv_refs = refs[6 + 2 * parts : 6 + 3 * parts]
    acc_ref = refs[6 + 3 * parts]
    n = q_ref.shape[0]
    seg = seg_ref[...]
    group = min(2, parts)
    for c in range(0, parts, group):
        k = jnp.concatenate([r[...] for r in k_refs[c : c + group]])
        v = jnp.concatenate([r[...] for r in v_refs[c : c + group]])
        ks = both_masks(k, jnp.concatenate([seg] * group))
        lk = lanes(k.shape) < HD
        z = jnp.zeros_like(k)
        km = [jnp.where(lk, k, z), jnp.where(lk, z, k)]
        dk = jnp.zeros(k.shape, f32)
        dv = jnp.zeros(k.shape, f32)
        for t in range(n // tq):
            rows = pl.ds(t * tq, tq)
            q = q_ref[rows, :] * jnp.asarray(0.125, bf)
            do = do_ref[rows, :]
            lq = lanes(q.shape) < HD
            zq = jnp.zeros_like(q)
            segq = seg_ref[rows, :]
            lse = lse_ref[rows, :]
            prod = do.astype(f32) * o_ref[rows, :].astype(f32)
            dqs = None
            for h in range(2):
                own = lq if h == 0 else ~lq
                qq = jnp.where(own, q, mask_feats_q(segq, HD if h == 0 else 0).astype(bf))
                qm = jnp.where(own, q, zq)
                dom = jnp.where(own, do, zq)
                dd = jnp.sum(jnp.where(own, prod, 0.0), axis=-1, keepdims=True)
                ls = lse[:, :1] if h == 0 else lse[:, HD : HD + 1]
                p = jnp.exp(nt(qq, ks[h]) - ls)
                ds = (p * (nt(dom, v) - dd)).astype(bf)
                dv = dv + tn(p.astype(bf), dom)
                dk = dk + tn(ds, qm)
                x = nn(ds, km[h])
                dqs = x if dqs is None else dqs + x
            if c == 0:
                acc_ref[rows, :] = dqs
            else:
                acc_ref[rows, :] += dqs
        for i in range(group):
            dkv_refs[c + i][0] = dk[i * n : (i + 1) * n].astype(bf)
            dkv_refs[c + i][1] = dv[i * n : (i + 1) * n].astype(bf)
    dq_ref[...] = (acc_ref[...] * 0.125).astype(bf)


def attn_bwd(q, blocks, do, o, lse, seg, first, count, tq=256):
    n = q.shape[0]
    parts, d = len(blocks), count * 2 * HD
    wide, key, val, one = specs(n, first, count)
    pair = pl.BlockSpec((2, n, 2 * HD), lambda h: (0, 0, h))
    return pl.pallas_call(
        functools.partial(bwd_kernel, tq=min(tq, n), parts=parts),
        grid=(count,),
        in_specs=[wide, wide, key, key, one] + [key] * parts + [val] * parts,
        out_specs=[key] + [pair] * parts,
        out_shape=[jax.ShapeDtypeStruct((n, d), bf)] + [jax.ShapeDtypeStruct((2, n, d), bf)] * parts,
        scratch_shapes=[pltpu.VMEM((n, 2 * HD), f32)],
        cost_estimate=pl.CostEstimate(
            flops=40 * n * n * parts * d, bytes_accessed=n * d * (12 + 8 * parts), transcendentals=0
        ),
        name="attn_bwd",
    )(q, do, o, lse, seg[:, None], *blocks, *blocks)


def normed(value, gain, shift):
    center = value - jnp.mean(value, axis=-1, keepdims=True)
    spread = jnp.mean(center * center, axis=-1, keepdims=True)
    return center * lax.rsqrt(spread + 1e-06) * gain + shift


GELU = (2 / math.pi) ** 0.5


def swap(x, flip):
    parts = lax.axis_size("band")
    return lax.ppermute(x, "band", [(i, i ^ flip) for i in range(parts)])


def spread(blocks, flip):
    while flip >= 1:
        blocks = blocks + [swap(block, flip) for block in blocks]
        flip //= 2
    return blocks


def tie(first, second):
    return lax.optimization_barrier((first, second))


def fold(blocks, flip):
    half = len(blocks) // 2
    return [
        (near.astype(f32) + swap(far, flip).astype(f32)).astype(bf)
        for near, far in zip(blocks[:half], blocks[half:])
    ]


def reduce_relative(blocks, flip=1):
    while len(blocks) > 1:
        blocks = fold(blocks, flip)
        flip *= 2
    return blocks[0]


def gather_vectors(shards):
    packed = jnp.concatenate(shards)
    whole = lax.all_gather(packed, "band", axis=0, tiled=False)
    out, at = [], 0
    for shard in shards:
        out.append(whole[:, at : at + shard.shape[0]].reshape(-1).astype(f32))
        at += shard.shape[0]
    return out


def relative_rows(array):
    me = lax.axis_index("band")
    order = [0]
    flip = lax.axis_size("band") // 2
    while flip >= 1:
        order = order + [i ^ flip for i in order]
        flip //= 2
    return [lax.dynamic_index_in_dim(array, me ^ i, 0, keepdims=False) for i in order]


def reduce_last(matrix, grads, shards):
    parts, columns = lax.axis_size("band"), matrix.shape[1]
    packed = jnp.concatenate([g.reshape(parts, -1) for g in grads], axis=1).astype(bf)
    rows = -(-packed.shape[1] // (16 * columns)) * 16
    packed = jnp.pad(packed, ((0, 0), (0, rows * columns - packed.shape[1])))
    mine = reduce_chip(reduce_core(matrix))
    extra = reduce_relative(relative_rows(packed.reshape(parts, rows, columns)))
    vector = sum_small(extra).reshape(-1)
    total = finish(mine, 1)
    out, at = [], 0
    for shard in shards:
        out.append(vector[at : at + shard.shape[0]])
        at += shard.shape[0]
    return total, out


def gather_matrix(shard):
    return lax.all_gather(shard, "band", axis=0, tiled=True)


def reduce_core(grad):
    blocks = grad.reshape(lax.axis_size("band"), -1, grad.shape[1])
    return fold(relative_rows(blocks), 1)


def reduce_chip(blocks):
    return reduce_relative(blocks, 2)


def trade(x, flip):
    size = lax.axis_size("dp")
    return lax.ppermute(x, "dp", [(i, i ^ flip) for i in range(size)])


def halve(x, flip):
    bit = lax.rem(lax.axis_index("dp") // flip, 2)
    halves = x.reshape(2, -1, x.shape[1])
    near = lax.dynamic_index_in_dim(halves, bit, 0, keepdims=False)
    far = lax.dynamic_index_in_dim(halves, 1 - bit, 0, keepdims=False)
    return (near.astype(f32) + trade(far, flip).astype(f32)).astype(bf)


def join(x, flip):
    bit = lax.rem(lax.axis_index("dp") // flip, 2)
    other = trade(x, flip)
    return jnp.where(bit == 0, jnp.concatenate([x, other]), jnp.concatenate([other, x]))


def finish(x, flip):
    size = lax.axis_size("dp")
    while flip < size:
        x = halve(x, flip)
        flip *= 2
    while flip > 1:
        flip //= 2
        x = join(x, flip)
    return x.astype(f32)


def sum_small(x):
    flip = 1
    while flip < lax.axis_size("dp"):
        x = (x.astype(f32) + trade(x, flip).astype(f32)).astype(bf)
        flip *= 2
    return x.astype(f32)


def layer(inputs, segments, cotangent, ln1_gain, ln1_bias, w_qkv, b_qv, w_out, b_out, ln2_gain, ln2_bias, w_up, b_up, w_down, b_down):
    micro, tokens, width = inputs.shape[0], inputs.shape[2], inputs.shape[3]
    parts = lax.axis_size("band")
    vectors = (ln1_gain, ln1_bias, b_qv, b_out, ln2_gain, ln2_bias, b_up, b_down)
    gain_one, shift_one, bias_qv, bias_out, gain_two, shift_two, bias_up, bias_down = gather_vectors(vectors)
    w_proj = gather_matrix(w_qkv)

    value = inputs.reshape(micro * tokens, width).astype(f32)
    seg = segments.reshape(micro, tokens)
    normed_in, pull_one = jax.vjp(normed, value, gain_one, shift_one)
    normed_low = normed_in.astype(bf)
    projected = nn(normed_low, w_proj)
    query = (projected[:, :width] + bias_qv[:width]).astype(bf)
    keys = projected[:, width : 2 * width].astype(bf)
    values = (projected[:, 2 * width :] + bias_qv[width:]).astype(bf)

    count = width // (4 * HD)
    half = width // 2
    far = parts // 2
    units = [(m, first) for m in range(micro) for first in (0, count)]
    started = []
    for i, (m, first) in enumerate(units):
        rows, cols = slice(m * tokens, (m + 1) * tokens), slice(first * 2 * HD, first * 2 * HD + half)
        own = jnp.concatenate([keys[rows, cols], values[rows, cols]], axis=1)
        if i > 0:
            started[i - 1], own = tie(started[i - 1], own)
        started.append(own)
    for i, own in enumerate(started):
        started[i] = [own, swap(own, far)]

    saved, mixes = [], []
    for i, (m, first) in enumerate(units):
        blocks = started[i]
        if i > 0:
            blocks, mixes[i - 1] = tie(blocks, mixes[i - 1])
        blocks = spread(blocks, far // 2)
        if i == 0:
            blocks, (w_out, w_up, w_down) = tie(blocks, (w_out, w_up, w_down))
            w_mix = gather_matrix(w_out)
            w_rise = gather_matrix(w_up)
            w_fall = gather_matrix(w_down)
        q = query[m * tokens : (m + 1) * tokens]
        mix, log_total = attn_fwd(q, blocks, seg[m], first, count)
        mixes.append(mix)
        saved.append((q, blocks, mix, log_total, seg[m]))
    mixed = jnp.concatenate(
        [jnp.concatenate(mixes[i : i + 2], axis=1) for i in range(0, 2 * micro, 2)]
    )

    hidden = value + (nn(mixed, w_mix) + bias_out)
    normed_mid, pull_two = jax.vjp(normed, hidden, gain_two, shift_two)
    mid_low = normed_mid.astype(bf)
    upward = nn(mid_low, w_rise) + bias_up
    bent = jnp.tanh(GELU * (upward + 0.044715 * upward * upward * upward))
    active_low = (0.5 * upward * (1 + bent)).astype(bf)
    slope = 0.5 * (1 + bent) + 0.5 * upward * (1 - bent * bent) * (GELU * (1 + 3 * 0.044715 * upward * upward))
    active_low, slope = lax.optimization_barrier((active_low, slope))

    real = (seg.reshape(-1, 1) != 0).astype(f32)
    grad_y = cotangent.reshape(micro * tokens, width).astype(f32) * real
    grad_m = grad_y.astype(bf)
    grad_w_fall = tn(active_low, grad_m)
    grad_b_fall = jnp.sum(grad_m.astype(f32), axis=0)
    low_fall, grad_m = tie(grad_w_fall.astype(bf), grad_m)
    fall = reduce_core(low_fall)
    grad_up = (nt(grad_m, w_fall) * slope).astype(bf)
    fall, grad_up = tie(fall, grad_up)
    fall = reduce_chip(fall)
    grad_w_rise = tn(mid_low, grad_up)
    low_rise, grad_up = tie(grad_w_rise.astype(bf), grad_up)
    rise = reduce_core(low_rise)
    grad_mid, grad_gain_two, grad_shift_two = pull_two(nt(grad_up, w_rise))
    grad_hidden = grad_y + grad_mid
    grad_a = grad_hidden.astype(bf)
    grad_w_mix = tn(mixed, grad_a)
    grad_b_mix = jnp.sum(grad_a.astype(f32), axis=0)
    grad_mixed = nt(grad_a, w_mix).astype(bf)

    (rise, low_out), grad_mixed = tie((rise, grad_w_mix.astype(bf)), grad_mixed)
    rise, out_grad = reduce_chip(rise), reduce_core(low_out)

    halves, grads_q = [], []
    for i, (m, first) in enumerate(units):
        q, blocks, mix, log_total, seg_q = saved[i]
        grad_out = grad_mixed[m * tokens : (m + 1) * tokens]
        if i >= 2:
            halves[i - 2], grad_out = tie(halves[i - 2], grad_out)
        if i == 1:
            (fall, out_grad), grad_out = tie((fall, out_grad), grad_out)
            out_grad = reduce_chip(out_grad)
        if i == 3:
            (fall, rise, out_grad), grad_out = tie((fall, rise, out_grad), grad_out)
            wide = [lax.psum(part, "dp") for part in (fall, rise, out_grad)]
        grad_q, *grad_blocks = attn_bwd(q, blocks, grad_out, mix, log_total, seg_q, first, count)
        halves.append(fold(grad_blocks, 1))
        grads_q.append(grad_q)
    halves[-1], (active_low, grad_up) = tie(halves[-1], (active_low, grad_up))
    output = (hidden + (nn(active_low, w_fall) + bias_down)).astype(bf)
    grad_b_rise = jnp.sum(grad_up.astype(f32), axis=0)
    pairs = []
    for half in halves:
        pairs.append(reduce_relative(half, 2))
    pairs, grads_q = tie(pairs, grads_q)
    grad_qkv = jnp.concatenate(
        [
            jnp.concatenate(
                [grads_q[i], grads_q[i + 1], pairs[i][0], pairs[i + 1][0], pairs[i][1], pairs[i + 1][1]], axis=1
            )
            for i in range(0, 2 * micro, 2)
        ]
    )
    grad_qkv = lax.optimization_barrier(grad_qkv)
    wide = [part.astype(f32) for part in wide]
    grad_w_proj = tn(normed_low, grad_qkv)
    low_proj, grad_qkv = tie(grad_w_proj.astype(bf), grad_qkv)
    sums = jnp.sum(grad_qkv.astype(f32), axis=0)
    grad_b_proj = jnp.concatenate([sums[:width], sums[2 * width :]])
    grad_norm_in, grad_gain_one, grad_shift_one = pull_one(nt(grad_qkv, w_proj))
    input_grad = (grad_hidden + grad_norm_in).astype(bf)

    last, small = reduce_last(
        low_proj,
        (grad_gain_one, grad_shift_one, grad_b_proj, grad_b_mix, grad_gain_two, grad_shift_two, grad_b_rise, grad_b_fall),
        vectors,
    )
    return (
        output.reshape(inputs.shape),
        input_grad.reshape(inputs.shape),
        small[0],
        small[1],
        last,
        small[2],
        wide[2],
        small[3],
        small[4],
        small[5],
        wide[1],
        small[6],
        wide[0],
        small[7],
    )


def solution(mesh):
    split = P(None, "dp", "band", None)
    rows, vector = P("band", None), P("band")
    weights = (vector, vector, rows, vector, rows, vector, vector, vector, rows, vector, rows, vector)
    return jax.shard_map(
        layer,
        mesh=mesh,
        in_specs=(split, P(None, "dp", "band"), split) + weights,
        out_specs=(split, split) + weights,
        check_vma=False,
    )
```

```python
import functools
import math

import jax
import jax.numpy as jnp
from jax import lax
from jax.sharding import PartitionSpec as P
from jax.experimental import pallas as pl
from jax.experimental.pallas import tpu as pltpu
bf=jnp.bfloat16; f32=jnp.float32
HD=64


def nt(a,b): return lax.dot_general(a,b,(((1,),(1,)),((),())),preferred_element_type=f32)


def nn(a,b): return lax.dot_general(a,b,(((1,),(0,)),((),())),preferred_element_type=f32)


def tn(a,b): return lax.dot_general(a,b,(((0,),(0,)),((),())),preferred_element_type=f32)


def lanes(shape): return lax.broadcasted_iota(jnp.int32,shape,1)


NEG=-1e30


def mask_feats_q(seg, base):
    l=lanes((seg.shape[0],2*HD))
    return (l==seg+base).astype(f32)


def mask_feats_k(seg, base):
    l=lanes((seg.shape[0],2*HD))
    inr=(l>=base)&(l<base+8)
    return jnp.where(inr&(l!=seg+base),NEG,0.0)


def both_masks(k, segk):
    low = lanes(k.shape) < HD
    return [
        jnp.where(low, k, mask_feats_k(segk, HD).astype(bf)),
        jnp.where(low, mask_feats_k(segk, 0).astype(bf), k),
    ]


def fwd_kernel(*refs, tq, parts):
    q_ref, seg_ref = refs[0], refs[1]
    k_refs, v_refs = refs[2 : 2 + parts], refs[2 + parts : 2 + 2 * parts]
    o_ref, lse_ref = refs[2 + 2 * parts :]
    n = q_ref.shape[0]
    v = jnp.concatenate([r[...] for r in v_refs])
    seg = seg_ref[...]
    ks = [jnp.concatenate(x) for x in zip(*[both_masks(r[...], seg) for r in k_refs])]
    for t in range(n // tq):
        rows = pl.ds(t * tq, tq)
        q = q_ref[rows, :] * jnp.asarray(0.125, bf)
        lq = lanes(q.shape) < HD
        segq = seg_ref[rows, :]
        outs, lses = [], []
        for h in range(2):
            feats = mask_feats_q(segq, HD if h == 0 else 0).astype(bf)
            qq = jnp.where(lq, q, feats) if h == 0 else jnp.where(lq, feats, q)
            s = nt(qq, ks[h])
            m = jnp.max(s, axis=-1, keepdims=True)
            p = jnp.exp(s - m)
            l = jnp.sum(p, axis=-1, keepdims=True)
            o = nn(p.astype(bf), v)
            outs.append(o / l)
            lses.append(m + jnp.log(l))
        o_ref[rows, :] = jnp.where(lq, outs[0], outs[1]).astype(bf)
        lse_ref[rows, :] = jnp.where(
            lq, jnp.broadcast_to(lses[0], q.shape), jnp.broadcast_to(lses[1], q.shape)
        )


def specs(n, first, count):
    wide = pl.BlockSpec((n, 2 * HD), lambda h: (0, h + first))
    key = pl.BlockSpec((n, 2 * HD), lambda h: (0, h))
    val = pl.BlockSpec((n, 2 * HD), lambda h: (0, h + count))
    seg = pl.BlockSpec((n, 1), lambda h: (0, 0))
    return wide, key, val, seg


def attn_fwd(q, blocks, seg, first, count, tq=256):
    n = q.shape[0]
    parts, d = len(blocks), count * 2 * HD
    wide, key, val, one = specs(n, first, count)
    return pl.pallas_call(
        functools.partial(fwd_kernel, tq=min(tq, n), parts=parts),
        grid=(count,),
        in_specs=[wide, one] + [key] * parts + [val] * parts,
        out_specs=[key, key],
        out_shape=[jax.ShapeDtypeStruct((n, d), bf), jax.ShapeDtypeStruct((n, d), f32)],
        cost_estimate=pl.CostEstimate(
            flops=16 * n * n * parts * d, bytes_accessed=n * d * (8 + 4 * parts), transcendentals=0
        ),
        name="attn_fwd",
    )(q, seg[:, None], *blocks, *blocks)


def bwd_kernel(*refs, tq, parts):
    q_ref, do_ref, o_ref, lse_ref, seg_ref = refs[:5]
    k_refs, v_refs = refs[5 : 5 + parts], refs[5 + parts : 5 + 2 * parts]
    dq_ref = refs[5 + 2 * parts]
    dkv_refs = refs[6 + 2 * parts : 6 + 3 * parts]
    acc_ref = refs[6 + 3 * parts]
    n = q_ref.shape[0]
    seg = seg_ref[...]
    group = min(2, parts)
    for c in range(0, parts, group):
        k = jnp.concatenate([r[...] for r in k_refs[c : c + group]])
        v = jnp.concatenate([r[...] for r in v_refs[c : c + group]])
        ks = both_masks(k, jnp.concatenate([seg] * group))
        lk = lanes(k.shape) < HD
        z = jnp.zeros_like(k)
        km = [jnp.where(lk, k, z), jnp.where(lk, z, k)]
        dk = jnp.zeros(k.shape, f32)
        dv = jnp.zeros(k.shape, f32)
        for t in range(n // tq):
            rows = pl.ds(t * tq, tq)
            q = q_ref[rows, :] * jnp.asarray(0.125, bf)
            do = do_ref[rows, :]
            lq = lanes(q.shape) < HD
            zq = jnp.zeros_like(q)
            segq = seg_ref[rows, :]
            lse = lse_ref[rows, :]
            prod = do.astype(f32) * o_ref[rows, :].astype(f32)
            dqs = None
            for h in range(2):
                own = lq if h == 0 else ~lq
                qq = jnp.where(own, q, mask_feats_q(segq, HD if h == 0 else 0).astype(bf))
                qm = jnp.where(own, q, zq)
                dom = jnp.where(own, do, zq)
                dd = jnp.sum(jnp.where(own, prod, 0.0), axis=-1, keepdims=True)
                ls = lse[:, :1] if h == 0 else lse[:, HD : HD + 1]
                p = jnp.exp(nt(qq, ks[h]) - ls)
                ds = (p * (nt(dom, v) - dd)).astype(bf)
                dv = dv + tn(p.astype(bf), dom)
                dk = dk + tn(ds, qm)
                x = nn(ds, km[h])
                dqs = x if dqs is None else dqs + x
            if c == 0:
                acc_ref[rows, :] = dqs
            else:
                acc_ref[rows, :] += dqs
        for i in range(group):
            dkv_refs[c + i][0] = dk[i * n : (i + 1) * n].astype(bf)
            dkv_refs[c + i][1] = dv[i * n : (i + 1) * n].astype(bf)
    dq_ref[...] = (acc_ref[...] * 0.125).astype(bf)


def attn_bwd(q, blocks, do, o, lse, seg, first, count, tq=256):
    n = q.shape[0]
    parts, d = len(blocks), count * 2 * HD
    wide, key, val, one = specs(n, first, count)
    pair = pl.BlockSpec((2, n, 2 * HD), lambda h: (0, 0, h))
    return pl.pallas_call(
        functools.partial(bwd_kernel, tq=min(tq, n), parts=parts),
        grid=(count,),
        in_specs=[wide, wide, key, key, one] + [key] * parts + [val] * parts,
        out_specs=[key] + [pair] * parts,
        out_shape=[jax.ShapeDtypeStruct((n, d), bf)] + [jax.ShapeDtypeStruct((2, n, d), bf)] * parts,
        scratch_shapes=[pltpu.VMEM((n, 2 * HD), f32)],
        cost_estimate=pl.CostEstimate(
            flops=40 * n * n * parts * d, bytes_accessed=n * d * (12 + 8 * parts), transcendentals=0
        ),
        name="attn_bwd",
    )(q, do, o, lse, seg[:, None], *blocks, *blocks)


def normed(value, gain, shift):
    center = value - jnp.mean(value, axis=-1, keepdims=True)
    spread = jnp.mean(center * center, axis=-1, keepdims=True)
    return center * lax.rsqrt(spread + 1e-06) * gain + shift


GELU = (2 / math.pi) ** 0.5


def swap(x, flip):
    parts = lax.axis_size("band")
    return lax.ppermute(x, "band", [(i, i ^ flip) for i in range(parts)])


def spread(blocks, flip):
    while flip >= 1:
        blocks = blocks + [swap(block, flip) for block in blocks]
        flip //= 2
    return blocks


def tie(first, second):
    return lax.optimization_barrier((first, second))


def fold(blocks, flip):
    half = len(blocks) // 2
    return [
        (near.astype(f32) + swap(far, flip).astype(f32)).astype(bf)
        for near, far in zip(blocks[:half], blocks[half:])
    ]


def reduce_relative(blocks, flip=1):
    while len(blocks) > 1:
        blocks = fold(blocks, flip)
        flip *= 2
    return blocks[0]


def gather_vectors(shards):
    packed = jnp.concatenate(shards)
    whole = lax.all_gather(packed, "band", axis=0, tiled=False)
    out, at = [], 0
    for shard in shards:
        out.append(whole[:, at : at + shard.shape[0]].reshape(-1).astype(f32))
        at += shard.shape[0]
    return out


def relative_rows(array):
    me = lax.axis_index("band")
    order = [0]
    flip = lax.axis_size("band") // 2
    while flip >= 1:
        order = order + [i ^ flip for i in order]
        flip //= 2
    return [lax.dynamic_index_in_dim(array, me ^ i, 0, keepdims=False) for i in order]


def reduce_last(matrix, grads, shards, beside):
    parts, columns = lax.axis_size("band"), matrix.shape[1]
    packed = jnp.concatenate([g.reshape(parts, -1) for g in grads], axis=1).astype(bf)
    rows = -(-packed.shape[1] // (16 * columns)) * 16
    packed = jnp.pad(packed, ((0, 0), (0, rows * columns - packed.shape[1])))
    mine = reduce_chip(reduce_core(matrix))
    extra = reduce_relative(relative_rows(packed.reshape(parts, rows, columns)))
    vector = sum_small(extra).reshape(-1)
    total, beside = finish(mine, 1, beside)
    out, at = [], 0
    for shard in shards:
        out.append(vector[at : at + shard.shape[0]])
        at += shard.shape[0]
    return total, out, beside


def gather_matrix(shard):
    return lax.all_gather(shard, "band", axis=0, tiled=True)


def reduce_core(grad):
    blocks = grad.reshape(lax.axis_size("band"), -1, grad.shape[1])
    return fold(relative_rows(blocks), 1)


def reduce_chip(blocks):
    return reduce_relative(blocks, 2)


def trade(x, flip):
    size = lax.axis_size("dp")
    return lax.ppermute(x, "dp", [(i, i ^ flip) for i in range(size)])


def halve(x, flip):
    bit = lax.rem(lax.axis_index("dp") // flip, 2)
    halves = x.reshape(2, -1, x.shape[1])
    near = lax.dynamic_index_in_dim(halves, bit, 0, keepdims=False)
    far = lax.dynamic_index_in_dim(halves, 1 - bit, 0, keepdims=False)
    return (near.astype(f32) + trade(far, flip).astype(f32)).astype(bf)


def join(x, flip):
    bit = lax.rem(lax.axis_index("dp") // flip, 2)
    other = trade(x, flip)
    return jnp.where(bit == 0, jnp.concatenate([x, other]), jnp.concatenate([other, x]))


def finish(x, flip, beside):
    size = lax.axis_size("dp")
    while flip < size:
        x = halve(x, flip)
        flip *= 2
    x, beside = tie(x, beside)
    while flip > 1:
        flip //= 2
        x = join(x, flip)
    return x.astype(f32), [part.astype(f32) for part in beside]


def sum_small(x):
    flip = 1
    while flip < lax.axis_size("dp"):
        x = (x.astype(f32) + trade(x, flip).astype(f32)).astype(bf)
        flip *= 2
    return x.astype(f32)


def layer(inputs, segments, cotangent, ln1_gain, ln1_bias, w_qkv, b_qv, w_out, b_out, ln2_gain, ln2_bias, w_up, b_up, w_down, b_down):
    micro, tokens, width = inputs.shape[0], inputs.shape[2], inputs.shape[3]
    parts = lax.axis_size("band")
    vectors = (ln1_gain, ln1_bias, b_qv, b_out, ln2_gain, ln2_bias, b_up, b_down)
    gain_one, shift_one, bias_qv, bias_out, gain_two, shift_two, bias_up, bias_down = gather_vectors(vectors)
    w_proj = gather_matrix(w_qkv)

    value = inputs.reshape(micro * tokens, width).astype(f32)
    seg = segments.reshape(micro, tokens)
    normed_in, pull_one = jax.vjp(normed, value, gain_one, shift_one)
    normed_low = normed_in.astype(bf)
    projected = nn(normed_low, w_proj)
    query = (projected[:, :width] + bias_qv[:width]).astype(bf)
    keys = projected[:, width : 2 * width].astype(bf)
    values = (projected[:, 2 * width :] + bias_qv[width:]).astype(bf)

    count = width // (4 * HD)
    half = width // 2
    far = parts // 2
    units = [(m, first) for m in range(micro) for first in (0, count)]
    started = []
    for i, (m, first) in enumerate(units):
        rows, cols = slice(m * tokens, (m + 1) * tokens), slice(first * 2 * HD, first * 2 * HD + half)
        own = jnp.concatenate([keys[rows, cols], values[rows, cols]], axis=1)
        if i > 0:
            started[i - 1], own = tie(started[i - 1], own)
        started.append(own)
    for i, own in enumerate(started):
        started[i] = [own, swap(own, far)]

    saved, mixes = [], []
    for i, (m, first) in enumerate(units):
        blocks = started[i]
        if i > 0:
            blocks, mixes[i - 1] = tie(blocks, mixes[i - 1])
        blocks = spread(blocks, far // 2)
        if i == 0:
            blocks, (w_out, w_up, w_down) = tie(blocks, (w_out, w_up, w_down))
            w_mix = gather_matrix(w_out)
            w_rise = gather_matrix(w_up)
            w_fall = gather_matrix(w_down)
        q = query[m * tokens : (m + 1) * tokens]
        mix, log_total = attn_fwd(q, blocks, seg[m], first, count)
        mixes.append(mix)
        saved.append((q, blocks, mix, log_total, seg[m]))
    mixed = jnp.concatenate(
        [jnp.concatenate(mixes[i : i + 2], axis=1) for i in range(0, 2 * micro, 2)]
    )

    hidden = value + (nn(mixed, w_mix) + bias_out)
    normed_mid, pull_two = jax.vjp(normed, hidden, gain_two, shift_two)
    mid_low = normed_mid.astype(bf)
    upward = nn(mid_low, w_rise) + bias_up
    bent = jnp.tanh(GELU * (upward + 0.044715 * upward * upward * upward))
    active_low = (0.5 * upward * (1 + bent)).astype(bf)
    slope = 0.5 * (1 + bent) + 0.5 * upward * (1 - bent * bent) * (GELU * (1 + 3 * 0.044715 * upward * upward))
    active_low, slope = lax.optimization_barrier((active_low, slope))

    real = (seg.reshape(-1, 1) != 0).astype(f32)
    grad_y = cotangent.reshape(micro * tokens, width).astype(f32) * real
    grad_m = grad_y.astype(bf)
    grad_w_fall = tn(active_low, grad_m)
    grad_b_fall = jnp.sum(grad_m.astype(f32), axis=0)
    low_fall, grad_m = tie(grad_w_fall.astype(bf), grad_m)
    fall = reduce_core(low_fall)
    grad_up = (nt(grad_m, w_fall) * slope).astype(bf)
    fall, grad_up = tie(fall, grad_up)
    fall = reduce_chip(fall)
    grad_w_rise = tn(mid_low, grad_up)
    low_rise, grad_up = tie(grad_w_rise.astype(bf), grad_up)
    rise = reduce_core(low_rise)
    grad_mid, grad_gain_two, grad_shift_two = pull_two(nt(grad_up, w_rise))
    grad_hidden = grad_y + grad_mid
    grad_a = grad_hidden.astype(bf)
    grad_w_mix = tn(mixed, grad_a)
    grad_b_mix = jnp.sum(grad_a.astype(f32), axis=0)
    grad_mixed = nt(grad_a, w_mix).astype(bf)

    (rise, low_out), grad_mixed = tie((rise, grad_w_mix.astype(bf)), grad_mixed)
    rise, out_grad = reduce_chip(rise), reduce_core(low_out)

    halves, grads_q = [], []
    for i, (m, first) in enumerate(units):
        q, blocks, mix, log_total, seg_q = saved[i]
        grad_out = grad_mixed[m * tokens : (m + 1) * tokens]
        if i >= 2:
            halves[i - 2], grad_out = tie(halves[i - 2], grad_out)
        if i == 1:
            (fall, out_grad), grad_out = tie((fall, out_grad), grad_out)
            out_grad = reduce_chip(out_grad)
        if i == 3:
            (fall, rise, out_grad), grad_out = tie((fall, rise, out_grad), grad_out)
            wide = [lax.psum(part, "dp") for part in (fall, rise, out_grad)]
        grad_q, *grad_blocks = attn_bwd(q, blocks, grad_out, mix, log_total, seg_q, first, count)
        halves.append(fold(grad_blocks, 1))
        grads_q.append(grad_q)
    grads_q[-2], (active_low, grad_up) = tie(grads_q[-2], (active_low, grad_up))
    output = (hidden + (nn(active_low, w_fall) + bias_down)).astype(bf)
    grad_b_rise = jnp.sum(grad_up.astype(f32), axis=0)
    pairs = []
    for half in halves:
        pairs.append(reduce_relative(half, 2))
    pairs, grads_q = tie(pairs, grads_q)
    grad_qkv = jnp.concatenate(
        [
            jnp.concatenate(
                [grads_q[i], grads_q[i + 1], pairs[i][0], pairs[i + 1][0], pairs[i][1], pairs[i + 1][1]], axis=1
            )
            for i in range(0, 2 * micro, 2)
        ]
    )
    grad_qkv = lax.optimization_barrier(grad_qkv)
    grad_w_proj = tn(normed_low, grad_qkv)
    low_proj, grad_qkv = tie(grad_w_proj.astype(bf), grad_qkv)
    sums = jnp.sum(grad_qkv.astype(f32), axis=0)
    grad_b_proj = jnp.concatenate([sums[:width], sums[2 * width :]])
    grad_norm_in, grad_gain_one, grad_shift_one = pull_one(nt(grad_qkv, w_proj))
    input_grad = (grad_hidden + grad_norm_in).astype(bf)

    last, small, wide = reduce_last(
        low_proj,
        (grad_gain_one, grad_shift_one, grad_b_proj, grad_b_mix, grad_gain_two, grad_shift_two, grad_b_rise, grad_b_fall),
        vectors,
        wide,
    )
    return (
        output.reshape(inputs.shape),
        input_grad.reshape(inputs.shape),
        small[0],
        small[1],
        last,
        small[2],
        wide[2],
        small[3],
        small[4],
        small[5],
        wide[1],
        small[6],
        wide[0],
        small[7],
    )


def solution(mesh):
    split = P(None, "dp", "band", None)
    rows, vector = P("band", None), P("band")
    weights = (vector, vector, rows, vector, rows, vector, vector, vector, rows, vector, rows, vector)
    return jax.shard_map(
        layer,
        mesh=mesh,
        in_specs=(split, P(None, "dp", "band"), split) + weights,
        out_specs=(split, split) + weights,
        check_vma=False,
    )
```
